32 devices in a mesh: dp: 4 (over x, core), fsdp: 8 (over z, y).
Axes of the slice: x: 2, y: 2, z: 4, core: 2. Of those that a mesh axis runs over, the one named last changes fastest.
Arguments:
- tokens: bfloat16 [4096, 1280], P(('dp', 'fsdp')), may hold values from -6 to 6
- teacher: bfloat16 [4096, 1280], P(('dp', 'fsdp'))
- out_grad: bfloat16 [4096, 1280], P(('dp', 'fsdp')), may hold values from -6 to 6
- attn_gain: bfloat16 [1280], P(('dp', 'fsdp')), may hold values from 0.5 to 1.5
- w_query: bfloat16 [1280, 1024], P(('dp', 'fsdp')), may hold values from -0.15625 to 0.15625
- w_key: bfloat16 [1280, 256], P(('dp', 'fsdp')), may hold values from -0.15625 to 0.15625
- w_value: bfloat16 [1280, 256], P(('dp', 'fsdp')), may hold values from -0.15625 to 0.15625
- w_out: bfloat16 [1024, 1280], P(('dp', 'fsdp')), may hold values from -1.5 to 1.5
- query_gain: bfloat16 [64], replicated, may hold values from 0.5 to 1.5
- key_gain: bfloat16 [64], replicated, may hold values from 0.5 to 1.5
- ffn_gain: bfloat16 [1280], P(('dp', 'fsdp')), may hold values from 0.5 to 1.5
- w_gate: bfloat16 [1280, 3072], P(('dp', 'fsdp')), may hold values from -0.15625 to 0.15625
- w_up: bfloat16 [1280, 3072], P(('dp', 'fsdp')), may hold values from -0.15625 to 0.15625
- w_down: bfloat16 [3072, 1280], P(('dp', 'fsdp')), may hold values from -0.109375 to 0.109375
- seq_lengths: int32 [32, 4], replicated, may hold values from 1 to 96, as said below
- send_order: int32 [32, 128], P(('dp', 'fsdp')), may hold values from 0 to 127, each once within a row
- pack_order: int32 [32, 128], P(('dp', 'fsdp')), may hold values from 0 to 127, each once within a row
Outputs:
- mixed: bfloat16 [4096, 1280], P(('dp', 'fsdp'))
- loss: float32 [], replicated
- input_grad: float32 [4096, 1280], P(('dp', 'fsdp'))
- attn_gain_grad: float32 [1280], P(('dp', 'fsdp'))
- w_query_grad: float32 [1280, 1024], P(('dp', 'fsdp'))
- w_key_grad: float32 [1280, 256], P(('dp', 'fsdp'))
- w_value_grad: float32 [1280, 256], P(('dp', 'fsdp'))
- w_out_grad: float32 [1024, 1280], P(('dp', 'fsdp'))
- query_gain_grad: float32 [64], replicated
- key_gain_grad: float32 [64], replicated
- ffn_gain_grad: float32 [1280], P(('dp', 'fsdp'))
- w_gate_grad: float32 [1280, 3072], P(('dp', 'fsdp'))
- w_up_grad: float32 [1280, 3072], P(('dp', 'fsdp'))
- w_down_grad: float32 [3072, 1280], P(('dp', 'fsdp'))
The draws below stay inside these ranges and needn't reach their ends.
Inputs may be any that keep to these rules, and one draw needn't show every extreme that they name: `seq_lengths`: each row holds the lengths of one device's 4 sequences in packing order; exactly one of them is 96, the others lie between 1 and 10. `send_order`: each row is an order of the 128 loader rows of one device. `pack_order`: each row is an order of the 128 received positions of one device.
All inputs are finite; a program needn't handle non-finite values.
Results may differ from the reference program's by a relative error of at most 0.012.
Values may be sent and summed in bfloat16 or wider, within the bound.
No kernel may reach another device: no remote copies, remote signals or barrier semaphores. Data moves between devices by JAX's collectives and lax.ppermute only.
A program may use at most 192 MiB of HBM per device.

```python
import jax
import jax.numpy as jnp
from jax import lax

D = 1280
HEADS = 16
KV_HEADS = 4
HD = 64
FF = 3072
TOK_DEV = 128
SEQ_DEV = 4
LONGEST = 96
QW = 1024
KVW = 256
TOKENS = 4096
N_DP = 4
N_FSDP = 8


def draw_teacher(key, part):
    device_pos = (jnp.arange(TOKENS, dtype=jnp.int32) // TOK_DEV).astype(jnp.float32)
    last_dev = max(TOKENS // TOK_DEV - 1, 1)
    ramp = device_pos / last_dev
    base = jax.random.normal(jax.random.fold_in(key, 11), (TOKENS, D), jnp.float32)
    scale_rows = 1.0 + 2.0 * ramp
    return (base * scale_rows[:, None]).astype(jnp.bfloat16)


def draw_seq_lengths(key, part):
    devices = TOKENS // TOK_DEV
    short_most = (TOK_DEV - LONGEST) // (SEQ_DEV - 1)
    short_rows = jax.random.randint(jax.random.fold_in(key, 21), (devices, SEQ_DEV), 1, short_most + 1)
    long_slot = jax.random.randint(jax.random.fold_in(key, 22), (devices, 1), 0, SEQ_DEV)
    slots = jnp.arange(SEQ_DEV, dtype=jnp.int32)[None, :]
    return jnp.where(slots == long_slot, LONGEST, short_rows).astype(jnp.int32)


def steps_of(stream_key, shape, pieces, least, top_value):
    gain = 1.0
    for dim, blocks in pieces:
        heights = jax.random.uniform(jax.random.fold_in(jax.random.fold_in(stream_key, 6), dim), (blocks,), jnp.float32, least / len(pieces), top_value / len(pieces))
        gain = gain * jnp.repeat(jnp.exp(heights), shape[dim] // blocks).reshape((-1,) + (1,) * (len(shape) - 1 - dim))
    return gain


def gaussian(key, extent, spread, reach, split=(), kind=jnp.bfloat16):
    gain = steps_of(key, extent, split, -0.22, 0.18) if split else 1.0
    array = jax.random.normal(key, extent, jnp.float32) * spread * gain
    return jnp.minimum(jnp.maximum(array, -reach), reach).astype(kind)


def setup_inputs(seed: int = 0) -> dict:
    key_of = jax.random.split(jax.random.key(seed), 18)
    tokens = gaussian(key_of[0], (TOKENS, D), 1.0, 6.0, ((0, 32),))
    teacher = draw_teacher(jax.random.fold_in(key_of[17], 71), 0)
    out_grad = gaussian(key_of[2], (TOKENS, D), 1.0, 6.0, ((0, 32),))
    attn_gain = jnp.clip(1.0 + 0.1 * jax.random.normal(key_of[3], (D,), jnp.float32), 0.5, 1.5).astype(jnp.bfloat16)
    w_query = gaussian(key_of[4], (D, QW), D ** -0.5, 0.15625, ((0, 32),))
    w_key = gaussian(key_of[5], (D, KVW), D ** -0.5, 0.15625, ((0, 32),))
    w_value = gaussian(key_of[6], (D, KVW), D ** -0.5, 0.15625, ((0, 32),))
    w_out = gaussian(key_of[7], (QW, D), (HEADS * HD // 64) ** -0.5, 1.5, ((0, 32),))
    query_gain = jnp.clip(1.0 + 0.1 * jax.random.normal(key_of[8], (HD,), jnp.float32), 0.5, 1.5).astype(jnp.bfloat16)
    key_gain = jnp.clip(1.0 + 0.1 * jax.random.normal(key_of[9], (HD,), jnp.float32), 0.5, 1.5).astype(jnp.bfloat16)
    ffn_gain = jnp.clip(1.0 + 0.1 * jax.random.normal(key_of[10], (D,), jnp.float32), 0.5, 1.5).astype(jnp.bfloat16)
    w_gate = gaussian(key_of[11], (D, FF), D ** -0.5, 0.15625, ((0, 32),))
    w_up = gaussian(key_of[12], (D, FF), D ** -0.5, 0.15625, ((0, 32),))
    w_down = gaussian(key_of[13], (FF, D), FF ** -0.5, 0.109375, ((0, 32),))
    seq_lengths = draw_seq_lengths(jax.random.fold_in(key_of[17], 71), 0)
    send_order = jax.vmap(lambda own: jax.random.permutation(own, TOK_DEV))(jax.random.split(key_of[15], (N_DP * N_FSDP))).reshape((N_DP * N_FSDP, TOK_DEV)).astype(jnp.int32)
    pack_order = jax.vmap(lambda own: jax.random.permutation(own, TOK_DEV))(jax.random.split(key_of[16], (N_DP * N_FSDP))).reshape((N_DP * N_FSDP, TOK_DEV)).astype(jnp.int32)
    return dict(tokens=tokens, teacher=teacher, out_grad=out_grad, attn_gain=attn_gain, w_query=w_query, w_key=w_key, w_value=w_value, w_out=w_out, query_gain=query_gain, key_gain=key_gain, ffn_gain=ffn_gain, w_gate=w_gate, w_up=w_up, w_down=w_down, seq_lengths=seq_lengths, send_order=send_order, pack_order=pack_order)


@jax.custom_vjp
def low(v):
    return lax.optimization_barrier(v.astype(jnp.bfloat16)).astype(jnp.float32)

@jax.custom_vjp
def low_back(v):
    return v

def low_keep(v):
    return (low(v), None)

def low_pass(kept, grad):
    return (grad,)

def back_keep(v):
    return (v, None)

def back_low(kept, grad):
    return (low(grad),)
low.defvjp(low_keep, low_pass)
low_back.defvjp(back_keep, back_low)
EPS = 1e-06
THETA = 10000.0
NEGATIVE = -1000000000.0
HIGHEST = lax.Precision.HIGHEST

def segment_info(lengths, row_count):
    seq_ends = jnp.cumsum(lengths).astype(jnp.int32)
    seq_starts = (seq_ends - lengths).astype(jnp.int32)
    row_index = jnp.arange(row_count, dtype=jnp.int32)
    segment = lax.optimization_barrier(jnp.sum((row_index[:, None] >= seq_ends[None, :]).astype(jnp.int32), axis=1)).astype(jnp.int32)
    seg_first = jnp.concatenate([seq_starts, seq_ends[-1:]]).astype(jnp.int32)
    labels = jnp.arange(seg_first.shape[0], dtype=jnp.int32)
    seg_begin = lax.optimization_barrier(jnp.sum(jnp.where(segment[:, None] == labels[None, :], seg_first[None, :], 0), axis=1)).astype(jnp.int32)
    allowed = (segment[:, None] == segment[None, :]) & (row_index[None, :] <= row_index[:, None])
    return ((row_index - seg_begin).astype(jnp.int32), allowed, segment < lengths.shape[0])

def norm_rows(values, gain_vec):
    return values * lax.rsqrt(lax.optimization_barrier(jnp.mean(values * values, axis=-1, keepdims=True)) + EPS) * gain_vec

def rope_tables(positions, head_width):
    half_width = head_width // 2
    frequency = THETA ** (-(jnp.arange(half_width, dtype=jnp.float32) * 2.0) / head_width)
    angles = positions.astype(jnp.float32)[:, None] * frequency[None, :]
    return (jnp.cos(angles), jnp.sin(angles))

def rotate(values, cosine, sine_table):
    half_width = values.shape[-1] // 2
    front_half = values[..., :half_width]
    second = values[..., half_width:]
    return jnp.concatenate([front_half * cosine - second * sine_table, front_half * sine_table + second * cosine], axis=-1)

def layer(weights_in, token_rows, lengths):
    row_count = token_rows.shape[0]
    positions, allowed, valid_rows = segment_info(lengths, row_count)
    cosine, sine_table = rope_tables(positions, HD)
    normed = low(norm_rows(token_rows, weights_in['attn_gain']))
    q_raw = low_back(jnp.dot(normed, weights_in['w_query'], precision=HIGHEST))
    k_raw = low_back(jnp.dot(normed, weights_in['w_key'], precision=HIGHEST))
    value_rows = low(low_back(jnp.dot(normed, weights_in['w_value'], precision=HIGHEST))).reshape(row_count, KV_HEADS, HD)
    query = norm_rows(q_raw.reshape(row_count, KV_HEADS, HEADS // KV_HEADS, HD), weights_in['query_gain'])
    key_rows = norm_rows(k_raw.reshape(row_count, KV_HEADS, HD), weights_in['key_gain'])
    query = low(rotate(query, cosine[:, None, None, :], sine_table[:, None, None, :]))
    key_rows = low(rotate(key_rows, cosine[:, None, :], sine_table[:, None, :]))
    raw_scores = jnp.einsum('rkgd,ckd->kgrc', query, key_rows, precision=HIGHEST) * HD ** (-0.5)
    scores = low_back(jnp.where(allowed[None, None], raw_scores, NEGATIVE))
    prob_rows = low(jax.nn.softmax(scores, axis=-1))
    heads_out = jnp.einsum('kgrc,ckd->rkgd', prob_rows, value_rows, precision=HIGHEST).reshape(row_count, HEADS * HD)
    heads_out = low(low_back(heads_out))
    hidden = token_rows + low_back(jnp.dot(heads_out, weights_in['w_out'], precision=HIGHEST))
    ffn_in = low(norm_rows(hidden, weights_in['ffn_gain']))
    gate_rows = low_back(jnp.dot(ffn_in, weights_in['w_gate'], precision=HIGHEST))
    up_rows = low_back(jnp.dot(ffn_in, weights_in['w_up'], precision=HIGHEST))
    act_rows = low(jax.nn.silu(gate_rows) * up_rows)
    result = hidden + low_back(jnp.dot(act_rows, weights_in['w_down'], precision=HIGHEST))
    return (low(result), valid_rows)

def reference(tokens, teacher, out_grad, attn_gain, w_query, w_key, w_value, w_out, query_gain, key_gain, ffn_gain, w_gate, w_up, w_down, seq_lengths, send_order, pack_order):
    devices = N_DP * N_FSDP
    piece_rows = TOK_DEV // N_FSDP
    device_ids = jnp.arange(devices, dtype=jnp.int32)
    source_dev = (device_ids // N_FSDP * N_FSDP)[:, None] + pack_order // piece_rows
    send_pos = (device_ids % N_FSDP)[:, None] * piece_rows + pack_order % piece_rows
    local_rows = send_order[source_dev, send_pos]
    whole_index = (source_dev * TOK_DEV + local_rows).reshape(-1).astype(jnp.int32)
    weights_in = {'attn_gain': attn_gain.astype(jnp.float32), 'w_query': w_query.astype(jnp.float32), 'w_key': w_key.astype(jnp.float32), 'w_value': w_value.astype(jnp.float32), 'w_out': w_out.astype(jnp.float32), 'query_gain': query_gain.astype(jnp.float32), 'key_gain': key_gain.astype(jnp.float32), 'ffn_gain': ffn_gain.astype(jnp.float32), 'w_gate': w_gate.astype(jnp.float32), 'w_up': w_up.astype(jnp.float32), 'w_down': w_down.astype(jnp.float32)}
    packed = tokens.astype(jnp.float32)[whole_index]
    target = teacher.astype(jnp.float32)[whole_index]
    seed_rows = out_grad.astype(jnp.float32)[whole_index]
    block_devs = 1
    while block_devs * 2 * TOK_DEV <= 4096 and devices % (block_devs * 2) == 0:
        block_devs = block_devs * 2
    scan_steps = devices // block_devs
    valid_count = jnp.sum(seq_lengths).astype(jnp.float32)
    length_blocks = seq_lengths.reshape(scan_steps, block_devs, SEQ_DEV)
    target_blocks = target.reshape(scan_steps, block_devs, TOK_DEV, D)

    def forward(weights_now, all_rows):

        def one_block(running, inputs):
            block_rows, block_target, block_lengths = inputs
            block_out, block_valid = jax.vmap(lambda rows_in, lengths_in: layer(weights_now, rows_in, lengths_in))(block_rows, block_lengths)
            row_error = block_out - block_target
            part_sum = jnp.sum(jnp.where(block_valid, lax.optimization_barrier(jnp.mean(row_error * row_error, axis=-1)), 0.0))
            return (running + part_sum, block_out)
        running, outputs = lax.scan(jax.checkpoint(one_block), jnp.zeros((), jnp.float32), (all_rows.reshape(scan_steps, block_devs, TOK_DEV, D), target_blocks, length_blocks))
        return (outputs.reshape(-1, D), running / valid_count)
    (packed_out, loss_total), pullback = jax.vjp(forward, weights_in, packed)
    loss_weight = jnp.asarray(TOKENS * D / 2.0, jnp.float32)
    weight_grads, packed_grad = pullback((seed_rows, loss_weight))
    mixed = jnp.zeros((TOKENS, D), jnp.float32).at[whole_index].set(packed_out)
    input_grad = jnp.zeros((TOKENS, D), jnp.float32).at[whole_index].set(packed_grad)
    return (mixed.astype(jnp.bfloat16), loss_total, input_grad, weight_grads['attn_gain'], weight_grads['w_query'], weight_grads['w_key'], weight_grads['w_value'], weight_grads['w_out'], weight_grads['query_gain'], weight_grads['key_gain'], weight_grads['ffn_gain'], weight_grads['w_gate'], weight_grads['w_up'], weight_grads['w_down'])
```

```python
import jax
import jax.numpy as jnp
from jax import lax
from jax.sharding import PartitionSpec as P

KV_HEADS = 4
HD = 64
TP = 4
AXES = ("dp", "fsdp")

EPS = 1e-06
THETA = 10000.0
NEGATIVE = -1000000000.0

BF16 = jnp.bfloat16
F32 = jnp.float32


def segment_info(lengths, row_count):
    seq_ends = jnp.cumsum(lengths)
    seq_starts = seq_ends - lengths
    row_index = jnp.arange(row_count, dtype=jnp.int32)
    segment = jnp.sum((row_index[:, None] >= seq_ends[None, :]).astype(jnp.int32), axis=1)
    seg_first = jnp.concatenate([seq_starts, seq_ends[-1:]])
    labels = jnp.arange(seg_first.shape[0], dtype=jnp.int32)
    seg_begin = jnp.sum(
        jnp.where(segment[:, None] == labels[None, :], seg_first[None, :], 0), axis=1
    )
    allowed = (segment[:, None] == segment[None, :]) & (row_index[None, :] <= row_index[:, None])
    return (row_index - seg_begin, allowed, segment < lengths.shape[0])


def norm_rows(values, gain_vec):
    return values * lax.rsqrt(jnp.mean(values * values, axis=-1, keepdims=True) + EPS) * gain_vec


def rope_tables(positions, head_width):
    half_width = head_width // 2
    frequency = THETA ** (-(jnp.arange(half_width, dtype=F32) * 2.0) / head_width)
    angles = positions.astype(F32)[:, None] * frequency[None, :]
    return (jnp.cos(angles), jnp.sin(angles))


def rotate(values, cosine, sine_table):
    half_width = values.shape[-1] // 2
    front_half = values[..., :half_width]
    second = values[..., half_width:]
    return jnp.concatenate(
        [front_half * cosine - second * sine_table, front_half * sine_table + second * cosine],
        axis=-1,
    )


def swiglu(gate_rows, up_rows):
    return jax.nn.silu(gate_rows) * up_rows


def dot(left, right):
    return jnp.dot(left, right, preferred_element_type=F32)


def dot_rows(left, right):
    return jnp.einsum("ra,rb->ab", left, right, preferred_element_type=F32)


def dot_back(left, right):
    return jnp.einsum("ra,ba->rb", left, right, preferred_element_type=F32)


class Layout:
    def __init__(self, devices):
        self.devices = devices
        self.ring = devices // TP
        evens = list(range(0, self.ring, 2))
        odds = list(range(1, self.ring, 2))
        self.cycle = evens + odds[::-1]
        self.place = [self.cycle.index(g) for g in range(self.ring)]
        self.me = lax.axis_index("dp") * lax.axis_size("fsdp") + lax.axis_index("fsdp")
        self.t = self.me // self.ring
        self.g = self.me % self.ring
        self.pos = jnp.asarray(self.place, jnp.int32)[self.g]

    def at(self, distance):
        index = lax.rem(self.pos + (distance + self.ring), self.ring)
        return jnp.asarray(self.cycle, jnp.int32)[index]

    def swap(self, value, bit):
        pairs = [
            (t * self.ring + g, (t ^ bit) * self.ring + g)
            for t in range(TP)
            for g in range(self.ring)
        ]
        return lax.ppermute(value, AXES, pairs)

    def shift(self, value, step):
        pairs = [
            (t * self.ring + g, t * self.ring + self.cycle[(self.place[g] + step) % self.ring])
            for t in range(TP)
            for g in range(self.ring)
        ]
        return lax.ppermute(value, AXES, pairs)

    def flip(self, value, bit):
        return lax.ppermute(value, AXES, [(n, n ^ bit) for n in range(self.devices)])

    def gather_tokens(self, own):
        core = self.swap(own, 1)
        across = self.swap(own, 2)
        far = self.swap(across, 1)
        return jnp.concatenate([own, core, across, far], axis=0)

    def scatter_tokens(self, part):
        blocks = part.reshape(TP, part.shape[0] // TP, part.shape[1])
        sent = jnp.concatenate([blocks[1], blocks[3]], axis=0).astype(BF16)
        got = self.swap(sent, 1).astype(F32).reshape(2, part.shape[0] // TP, part.shape[1])
        across = (blocks[2] + got[1]).astype(BF16)
        return blocks[0] + got[0] + self.swap(across, 2).astype(F32)

    def exchange(self, pieces):
        held = jnp.zeros_like(pieces)
        for bit in range(TP):
            piece = lax.dynamic_index_in_dim(pieces, self.t ^ bit, 0, keepdims=True)
            if bit:
                piece = self.swap(piece, bit)
            held = lax.dynamic_update_slice_in_dim(held, piece, self.t ^ bit, 0)
        return held

    def ring_gather(self, item, axis):
        shape = list(item.shape)
        shape[axis] = self.ring
        full = jnp.zeros(tuple(shape), item.dtype)
        full = lax.dynamic_update_slice_in_dim(full, item, self.g, axis)
        right = left = item
        last = self.ring // 2
        for step in range(1, last):
            right = self.shift(right, 1)
            left = self.shift(left, -1)
            full = lax.dynamic_update_slice_in_dim(full, right, self.at(-step), axis)
            full = lax.dynamic_update_slice_in_dim(full, left, self.at(step), axis)
        split = 0 if axis else 1
        half = item.shape[split] // 2
        first = self.shift(lax.slice_in_dim(right, 0, half, axis=split), 1)
        second = self.shift(lax.slice_in_dim(left, half, 2 * half, axis=split), -1)
        start = [jnp.int32(0)] * item.ndim
        start[axis] = self.at(last)
        full = lax.dynamic_update_slice(full, first, start)
        start[split] = jnp.int32(half)
        return lax.dynamic_update_slice(full, second, start)

    def ring_scatter(self, full, axis):
        def block(distance):
            return lax.dynamic_slice_in_dim(full, self.at(distance), 1, axis)

        split = 0 if axis else 1
        last = self.ring // 2
        edge = block(last)
        half = edge.shape[split] // 2
        right = self.shift(lax.slice_in_dim(edge, 0, half, axis=split), 1)
        left = self.shift(lax.slice_in_dim(edge, half, 2 * half, axis=split), -1)
        pad = [(0, 0, 0)] * edge.ndim
        pad[split] = (0, half, 0)
        right = lax.pad(right, jnp.zeros((), BF16), pad)
        pad[split] = (half, 0, 0)
        left = lax.pad(left, jnp.zeros((), BF16), pad)
        for step in range(last - 1, 0, -1):
            right = (block(step).astype(F32) + right.astype(F32)).astype(BF16)
            left = (block(-step).astype(F32) + left.astype(F32)).astype(BF16)
            right = self.shift(right, 1)
            left = self.shift(left, -1)
        return block(0).astype(F32) + right.astype(F32) + left.astype(F32)


def shards(
    tokens,
    teacher,
    out_grad,
    attn_gain,
    w_query,
    w_key,
    w_value,
    w_out,
    query_gain,
    key_gain,
    ffn_gain,
    w_gate,
    w_up,
    w_down,
    seq_lengths,
    send_order,
    pack_order,
):
    groups = lax.axis_size("fsdp")
    devices = lax.axis_size("dp") * groups
    lay = Layout(devices)
    ring = lay.ring
    rows = tokens.shape[0]
    width = tokens.shape[1]
    gain_rows = attn_gain.shape[0]
    q_cols = w_query.shape[1] // TP
    kv_cols = w_key.shape[1] // TP
    qkv_cols = q_cols + 2 * kv_cols
    heads = q_cols // HD
    ff_cols = w_gate.shape[1] // TP
    out_rows = w_out.shape[0]
    all_rows = TP * rows

    my_lengths = seq_lengths[lay.me]
    valid_count = jnp.sum(seq_lengths).astype(F32)
    loss_ratio = float(devices * rows) / valid_count
    send_rows = send_order[0]
    pack_rows = pack_order[0]
    counting = jnp.arange(rows, dtype=jnp.int32)
    send_back = jnp.zeros((rows,), jnp.int32).at[send_rows].set(counting)
    pack_back = jnp.zeros((rows,), jnp.int32).at[pack_rows].set(counting)

    def route(values):
        return lax.all_to_all(
            values[send_rows], "fsdp", split_axis=0, concat_axis=0, tiled=True
        )[pack_rows]

    def route_back(values):
        return lax.all_to_all(
            values[pack_back], "fsdp", split_axis=0, concat_axis=0, tiled=True
        )[send_back]

    pad_rows = 8
    qkv_pieces = jnp.concatenate(
        [
            w_query.reshape(gain_rows, TP, q_cols),
            w_key.reshape(gain_rows, TP, kv_cols),
            w_value.reshape(gain_rows, TP, kv_cols),
        ],
        axis=2,
    ).transpose(1, 0, 2)
    gain_line = jnp.concatenate(
        [
            jnp.pad(attn_gain, (0, 128 - gain_rows)),
            jnp.pad(ffn_gain, (0, 128 - gain_rows)),
            jnp.zeros((qkv_cols - 256,), BF16),
        ]
    )
    gain_block = jnp.broadcast_to(gain_line[None, None], (TP, pad_rows, qkv_cols))
    qkv_item = lay.exchange(jnp.concatenate([qkv_pieces, gain_block], axis=1))
    item_rows = TP * (gain_rows + pad_rows)
    out_item = w_out.reshape(out_rows, width // 256, 256).transpose(1, 0, 2)
    out_item = out_item.reshape(out_rows * (width // 256), 256)
    out_item = jnp.pad(out_item, ((0, item_rows - out_item.shape[0]), (0, 0)))
    attn_item = jnp.concatenate([qkv_item.reshape(item_rows, qkv_cols), out_item], axis=1)
    attn_full = lay.ring_gather(attn_item[None], 0)
    qkv_full = attn_full[:, :, :qkv_cols].reshape(ring, TP, gain_rows + pad_rows, qkv_cols)
    qkv_weight = qkv_full[:, :, :gain_rows].transpose(1, 0, 2, 3).reshape(width, qkv_cols)
    gain_full = qkv_full[:, :, gain_rows].transpose(1, 0, 2)
    attn_gain_all = gain_full[:, :, :gain_rows].reshape(width).astype(F32)
    ffn_gain_all = gain_full[:, :, 128 : 128 + gain_rows].reshape(width).astype(F32)
    out_weight = attn_full[:, : out_rows * (width // 256), qkv_cols:]
    out_weight = out_weight.reshape(ring, width // 256, out_rows, 256).transpose(0, 2, 1, 3)
    out_weight = out_weight.reshape(ring * out_rows, width)

    gate_up_pieces = jnp.concatenate(
        [w_gate.reshape(gain_rows, TP, ff_cols), w_up.reshape(gain_rows, TP, ff_cols)], axis=2
    ).transpose(1, 0, 2)
    gate_up_item = lay.exchange(gate_up_pieces)
    gate_up_weight = lay.ring_gather(gate_up_item[:, None], 1).reshape(width, 2 * ff_cols)
    down_weight = lay.ring_gather(w_down[None], 0).reshape(ff_cols, width)

    packed = route(tokens)
    teacher_rows = route(teacher)
    seed_rows = route(out_grad)
    inputs = packed.astype(F32)
    group_rows = lay.gather_tokens(packed)
    group_lengths = jnp.stack([seq_lengths[(lay.t ^ k) * ring + lay.g] for k in range(TP)])
    positions, allowed, valid_group = jax.vmap(lambda ls: segment_info(ls, rows))(group_lengths)
    valid_rows = valid_group[0].astype(F32)
    cosine, sine_table = rope_tables(positions.reshape(all_rows), HD)

    def prepare(q_raw, k_raw, q_scale, k_scale):
        query = norm_rows(q_raw.reshape(all_rows, heads, HD), q_scale)
        key_rows = norm_rows(k_raw, k_scale)
        query = rotate(query, cosine[:, None, :], sine_table[:, None, :])
        return (query, rotate(key_rows, cosine, sine_table))

    normed = norm_rows(group_rows.astype(F32), attn_gain_all).astype(BF16)
    qkv = dot(normed, qkv_weight)
    value_rows = qkv[:, q_cols + kv_cols :].astype(BF16).reshape(TP, rows, HD)
    (query_rot, key_rot), prepare_back = jax.vjp(
        prepare,
        qkv[:, :q_cols],
        qkv[:, q_cols : q_cols + kv_cols],
        query_gain.astype(F32),
        key_gain.astype(F32),
    )
    query_low = query_rot.astype(BF16).reshape(TP, rows, heads, HD)
    key_low = key_rot.astype(BF16).reshape(TP, rows, HD)
    scores = (
        jnp.einsum("brhd,bcd->bhrc", query_low, key_low, preferred_element_type=F32) * HD**-0.5
    )
    scores = jnp.where(allowed[:, None], scores, NEGATIVE)
    log_total = jax.nn.logsumexp(scores, axis=-1)
    prob_rows = jnp.exp(scores - log_total[..., None])
    prob_low = prob_rows.astype(BF16)
    heads_out = jnp.einsum("bhrc,bcd->brhd", prob_low, value_rows, preferred_element_type=F32)
    heads_out = heads_out.reshape(all_rows, q_cols).astype(BF16)
    hidden = inputs + lay.scatter_tokens(dot(heads_out, out_weight))
    ffn_own, ffn_norm_back = jax.vjp(norm_rows, hidden, ffn_gain_all)
    ffn_in = lay.gather_tokens(ffn_own.astype(BF16))
    gate_up = dot(ffn_in, gate_up_weight)
    act_value, act_back = jax.vjp(swiglu, gate_up[:, :ff_cols], gate_up[:, ff_cols:])
    act_low = act_value.astype(BF16)
    result = hidden + lay.scatter_tokens(dot(act_low, down_weight))
    result_low = result.astype(BF16)

    row_error = result_low.astype(F32) - teacher_rows.astype(F32)
    loss_part = jnp.sum(valid_rows * jnp.mean(row_error * row_error, axis=-1))
    upstream = seed_rows.astype(F32) + loss_ratio * valid_rows[:, None] * row_error
    upstream_low = lay.gather_tokens(upstream.astype(BF16))

    act_grad = dot_back(upstream_low, down_weight)
    down_grad = dot_rows(act_low, upstream_low).astype(BF16)
    gate_grad, up_grad = act_back(act_grad)
    gate_up_low = jnp.concatenate([gate_grad.astype(BF16), up_grad.astype(BF16)], axis=1)
    gate_up_grad = dot_rows(ffn_in, gate_up_low).astype(BF16)
    ffn_in_grad = lay.scatter_tokens(dot_back(gate_up_low, gate_up_weight))
    hidden_part, ffn_gain_part = ffn_norm_back(ffn_in_grad)
    hidden_grad = upstream + hidden_part

    down_shard = lay.ring_scatter(down_grad.reshape(ring, ff_cols // ring, width), 0)[0]
    gate_up_sum = lay.ring_scatter(gate_up_grad.reshape(TP, ring, gain_rows, 2 * ff_cols), 1)

    hidden_low = lay.gather_tokens(hidden_grad.astype(BF16))
    out_w_grad = dot_rows(heads_out, hidden_low).astype(BF16)
    head_grad = dot_back(hidden_low, out_weight).astype(BF16).reshape(TP, rows, heads, HD)
    value_grad = jnp.einsum("bhrc,brhd->bcd", prob_low, head_grad, preferred_element_type=F32)
    prob_grad = jnp.einsum("brhd,bcd->bhrc", head_grad, value_rows, preferred_element_type=F32)
    score_grad = prob_rows * (prob_grad - jnp.sum(prob_rows * prob_grad, axis=-1, keepdims=True))
    score_low = score_grad.astype(BF16)
    query_grad = (
        jnp.einsum("bhrc,bcd->brhd", score_low, key_low, preferred_element_type=F32) * HD**-0.5
    )
    key_grad = (
        jnp.einsum("bhrc,brhd->bcd", score_low, query_low, preferred_element_type=F32) * HD**-0.5
    )
    q_raw_grad, k_raw_grad, q_gain_part, k_gain_part = prepare_back(
        (query_grad.reshape(all_rows, heads, HD), key_grad.reshape(all_rows, HD))
    )
    qkv_low = jnp.concatenate(
        [
            q_raw_grad.astype(BF16),
            k_raw_grad.astype(BF16),
            value_grad.astype(BF16).reshape(all_rows, HD),
        ],
        axis=1,
    )
    qkv_grad = dot_rows(normed, qkv_low).astype(BF16)
    normed_grad_part = dot_back(qkv_low, qkv_weight)

    attn_blocks = jnp.concatenate(
        [
            qkv_grad.reshape(TP, ring, gain_rows, qkv_cols)
            .transpose(1, 0, 2, 3)
            .reshape(ring, TP * gain_rows, qkv_cols),
            out_w_grad.reshape(ring, out_rows, width // 256, 256)
            .transpose(0, 2, 1, 3)
            .reshape(ring, out_rows * (width // 256), 256),
        ],
        axis=2,
    )
    attn_sum = lay.ring_scatter(attn_blocks, 0)[0]

    normed_grad = lay.scatter_tokens(normed_grad_part)
    unused, attn_norm_back = jax.vjp(norm_rows, inputs, attn_gain_all)
    input_part, attn_gain_part = attn_norm_back(normed_grad)
    packed_grad = hidden_grad + input_part

    small = jnp.stack(
        [
            attn_gain_part,
            ffn_gain_part,
            jnp.concatenate(
                [
                    q_gain_part,
                    k_gain_part,
                    loss_part[None],
                    jnp.zeros((width - 2 * HD - 1,), F32),
                ]
            ),
        ]
    )
    small = jnp.pad(small, ((0, 5), (0, 0)))
    bit = 1
    while bit < devices:
        small = small + lay.flip(small, bit)
        bit = bit * 2
    attn_gain_shard = lax.dynamic_slice_in_dim(small[0], lay.me * gain_rows, gain_rows)
    ffn_gain_shard = lax.dynamic_slice_in_dim(small[1], lay.me * gain_rows, gain_rows)

    qkv_shard = lay.exchange(
        attn_sum[:, :qkv_cols].reshape(TP, gain_rows, qkv_cols).astype(BF16)
    ).astype(F32)
    gate_up_shard = lay.exchange(
        gate_up_sum.reshape(TP, gain_rows, 2 * ff_cols).astype(BF16)
    ).astype(F32)

    def whole(part):
        return part.transpose(1, 0, 2).reshape(gain_rows, -1)

    out_shard = (
        attn_sum[:, qkv_cols:].reshape(width // 256, out_rows, 256).transpose(1, 0, 2)
    ).reshape(out_rows, width)
    return (
        route_back(result_low),
        small[2, 2 * HD] / valid_count,
        route_back(packed_grad.astype(BF16)).astype(F32),
        attn_gain_shard,
        whole(qkv_shard[:, :, :q_cols]),
        whole(qkv_shard[:, :, q_cols : q_cols + kv_cols]),
        whole(qkv_shard[:, :, q_cols + kv_cols :]),
        out_shard,
        small[2, :HD],
        small[2, HD : 2 * HD],
        ffn_gain_shard,
        whole(gate_up_shard[:, :, :ff_cols]),
        whole(gate_up_shard[:, :, ff_cols:]),
        down_shard,
    )


def solution(mesh):
    rows = P(AXES, None)
    flat = P(AXES)
    in_specs = (rows, rows, rows, flat, rows, rows, rows, rows, P(), P(), flat)
    in_specs = in_specs + (rows, rows, rows, P(), rows, rows)
    out_specs = (rows, P(), rows, flat, rows, rows, rows, rows, P(), P(), flat, rows, rows, rows)
    return jax.shard_map(shards, mesh=mesh, in_specs=in_specs, out_specs=out_specs, check_vma=False)
```

```python
import jax
import jax.numpy as jnp
from jax import lax
from jax.sharding import PartitionSpec as P

KV_HEADS = 4
HD = 64
TP = 4
AXES = ("dp", "fsdp")

EPS = 1e-06
THETA = 10000.0
NEGATIVE = -1000000000.0

BF16 = jnp.bfloat16
F32 = jnp.float32


def segment_info(lengths, row_count):
    seq_ends = jnp.cumsum(lengths)
    seq_starts = seq_ends - lengths
    row_index = jnp.arange(row_count, dtype=jnp.int32)
    segment = jnp.sum((row_index[:, None] >= seq_ends[None, :]).astype(jnp.int32), axis=1)
    seg_first = jnp.concatenate([seq_starts, seq_ends[-1:]])
    labels = jnp.arange(seg_first.shape[0], dtype=jnp.int32)
    seg_begin = jnp.sum(
        jnp.where(segment[:, None] == labels[None, :], seg_first[None, :], 0), axis=1
    )
    allowed = (segment[:, None] == segment[None, :]) & (row_index[None, :] <= row_index[:, None])
    return (row_index - seg_begin, allowed, segment < lengths.shape[0])


def norm_rows(values, gain_vec):
    return values * lax.rsqrt(jnp.mean(values * values, axis=-1, keepdims=True) + EPS) * gain_vec


def rope_tables(positions, head_width):
    half_width = head_width // 2
    frequency = THETA ** (-(jnp.arange(half_width, dtype=F32) * 2.0) / head_width)
    angles = positions.astype(F32)[:, None] * frequency[None, :]
    return (jnp.cos(angles), jnp.sin(angles))


def rotate(values, cosine, sine_table):
    half_width = values.shape[-1] // 2
    front_half = values[..., :half_width]
    second = values[..., half_width:]
    return jnp.concatenate(
        [front_half * cosine - second * sine_table, front_half * sine_table + second * cosine],
        axis=-1,
    )


def swiglu(gate_rows, up_rows):
    return jax.nn.silu(gate_rows) * up_rows


def dot(left, right):
    return jnp.dot(left, right, preferred_element_type=F32)


def dot_rows(left, right):
    return jnp.einsum("ra,rb->ab", left, right, preferred_element_type=F32)


def dot_back(left, right):
    return jnp.einsum("ra,ba->rb", left, right, preferred_element_type=F32)


class Layout:
    def __init__(self, devices):
        self.devices = devices
        self.ring = devices // TP
        evens = list(range(0, self.ring, 2))
        odds = list(range(1, self.ring, 2))
        self.cycle = evens + odds[::-1]
        self.place = [self.cycle.index(g) for g in range(self.ring)]
        self.me = lax.axis_index("dp") * lax.axis_size("fsdp") + lax.axis_index("fsdp")
        self.t = self.me // self.ring
        self.g = self.me % self.ring
        half = self.g // 2
        self.pos = jnp.where(self.g == 2 * half, half, self.ring - 1 - half)

    def at(self, distance):
        index = self.pos + (distance % self.ring)
        index = jnp.where(index < self.ring, index, index - self.ring)
        return jnp.minimum(2 * index, 2 * self.ring - 1 - 2 * index)

    def swap(self, value, bit):
        pairs = [
            (t * self.ring + g, (t ^ bit) * self.ring + g)
            for t in range(TP)
            for g in range(self.ring)
        ]
        return lax.ppermute(value, AXES, pairs)

    def shift(self, value, step):
        pairs = [
            (t * self.ring + g, t * self.ring + self.cycle[(self.place[g] + step) % self.ring])
            for t in range(TP)
            for g in range(self.ring)
        ]
        return lax.ppermute(value, AXES, pairs)

    def flip(self, value, bit):
        return lax.ppermute(value, AXES, [(n, n ^ bit) for n in range(self.devices)])

    def gather_tokens(self, own):
        across = self.swap(own, 2)
        core = self.swap(own, 1)
        far = self.swap(across, 1)
        return jnp.concatenate([own, across, core, far], axis=0)

    def scatter_tokens(self, product, rows):
        half = rows.shape[0] // 2
        own = half // 2
        sent = product(rows[half:]).astype(BF16)
        kept = product(rows[:half]) + self.swap(sent, 1).astype(F32)
        across = self.swap(kept[own:].astype(BF16), 2)
        return kept[:own] + across.astype(F32)

    def exchange(self, pieces):
        held = jnp.zeros_like(pieces)
        for bit in (2, 3, 1, 0):
            piece = lax.dynamic_index_in_dim(pieces, self.t ^ bit, 0, keepdims=True)
            if bit:
                piece = self.swap(piece, bit)
            held = lax.dynamic_update_slice_in_dim(held, piece, self.t ^ bit, 0)
        return held

    def ring_gather(self, item, axis):
        shape = list(item.shape)
        shape[axis] = self.ring
        full = jnp.zeros(tuple(shape), item.dtype)
        full = lax.dynamic_update_slice_in_dim(full, item, self.g, axis)
        right = left = item
        last = self.ring // 2
        for step in range(1, last):
            right = self.shift(right, 1)
            left = self.shift(left, -1)
            full = lax.dynamic_update_slice_in_dim(full, right, self.at(-step), axis)
            full = lax.dynamic_update_slice_in_dim(full, left, self.at(step), axis)
        split = 0 if axis else 1
        half = item.shape[split] // 2
        first = self.shift(lax.slice_in_dim(right, 0, half, axis=split), 1)
        second = self.shift(lax.slice_in_dim(left, half, 2 * half, axis=split), -1)
        start = [jnp.int32(0)] * item.ndim
        start[axis] = self.at(last)
        full = lax.dynamic_update_slice(full, first, start)
        start[split] = jnp.int32(half)
        return lax.dynamic_update_slice(full, second, start)

    def ring_scatter(self, full, axis):
        def block(distance):
            return lax.dynamic_slice_in_dim(full, self.at(distance), 1, axis)

        split = 0 if axis else 1
        last = self.ring // 2
        edge = block(last)
        half = edge.shape[split] // 2
        right = self.shift(lax.slice_in_dim(edge, 0, half, axis=split), 1)
        left = self.shift(lax.slice_in_dim(edge, half, 2 * half, axis=split), -1)
        pad = [(0, 0, 0)] * edge.ndim
        pad[split] = (0, half, 0)
        right = lax.pad(right, jnp.zeros((), BF16), pad)
        pad[split] = (half, 0, 0)
        left = lax.pad(left, jnp.zeros((), BF16), pad)
        for step in range(last - 1, 0, -1):
            right = (block(step).astype(F32) + right.astype(F32)).astype(BF16)
            left = (block(-step).astype(F32) + left.astype(F32)).astype(BF16)
            right = self.shift(right, 1)
            left = self.shift(left, -1)
        return block(0).astype(F32) + right.astype(F32) + left.astype(F32)


def shards(
    tokens,
    teacher,
    out_grad,
    attn_gain,
    w_query,
    w_key,
    w_value,
    w_out,
    query_gain,
    key_gain,
    ffn_gain,
    w_gate,
    w_up,
    w_down,
    seq_lengths,
    send_order,
    pack_order,
):
    groups = lax.axis_size("fsdp")
    devices = lax.axis_size("dp") * groups
    lay = Layout(devices)
    ring = lay.ring
    rows = tokens.shape[0]
    width = tokens.shape[1]
    gain_rows = attn_gain.shape[0]
    q_cols = w_query.shape[1] // TP
    kv_cols = w_key.shape[1] // TP
    qkv_cols = q_cols + 2 * kv_cols
    heads = q_cols // HD
    ff_cols = w_gate.shape[1] // TP
    out_rows = w_out.shape[0]
    all_rows = TP * rows

    my_lengths = seq_lengths[lay.me]
    valid_count = jnp.sum(seq_lengths).astype(F32)
    loss_ratio = float(devices * rows) / valid_count
    send_rows = send_order[0]
    pack_rows = pack_order[0]
    counting = jnp.arange(rows, dtype=jnp.int32)
    send_pick = (send_rows[:, None] == counting[None, :]).astype(BF16)
    pack_pick = (pack_rows[:, None] == counting[None, :]).astype(BF16)

    def to_all(values):
        return lax.all_to_all(values, "fsdp", split_axis=0, concat_axis=0, tiled=True)

    def route(values):
        sent = to_all(dot(send_pick, values).astype(BF16))
        return dot(pack_pick, sent).astype(BF16)

    def route_back(values):
        sent = to_all(dot_rows(pack_pick, values).astype(BF16))
        return dot_rows(send_pick, sent)

    pad_rows = 8
    qkv_pieces = jnp.concatenate(
        [
            w_query.reshape(gain_rows, TP, q_cols),
            w_key.reshape(gain_rows, TP, kv_cols),
            w_value.reshape(gain_rows, TP, kv_cols),
        ],
        axis=2,
    ).transpose(1, 0, 2)
    gain_line = jnp.concatenate(
        [
            jnp.pad(attn_gain, (0, 128 - gain_rows)),
            jnp.pad(ffn_gain, (0, 128 - gain_rows)),
            jnp.zeros((qkv_cols - 256,), BF16),
        ]
    )
    gain_block = jnp.broadcast_to(gain_line[None, None], (TP, pad_rows, qkv_cols))
    qkv_item = lay.exchange(jnp.concatenate([qkv_pieces, gain_block], axis=1))
    item_rows = TP * (gain_rows + pad_rows)
    out_item = w_out.reshape(out_rows, width // 256, 256).transpose(1, 0, 2)
    out_item = out_item.reshape(out_rows * (width // 256), 256)
    out_item = jnp.pad(out_item, ((0, item_rows - out_item.shape[0]), (0, 0)))
    attn_item = jnp.concatenate([qkv_item.reshape(item_rows, qkv_cols), out_item], axis=1)
    attn_full = lay.ring_gather(attn_item[None], 0)
    qkv_full = attn_full[:, :, :qkv_cols].reshape(ring, TP, gain_rows + pad_rows, qkv_cols)
    qkv_weight = qkv_full[:, :, :gain_rows].transpose(1, 0, 2, 3).reshape(width, qkv_cols)
    gain_full = qkv_full[:, :, gain_rows].transpose(1, 0, 2)
    attn_gain_all = gain_full[:, :, :gain_rows].reshape(width).astype(F32)
    ffn_gain_all = gain_full[:, :, 128 : 128 + gain_rows].reshape(width).astype(F32)
    out_weight = attn_full[:, : out_rows * (width // 256), qkv_cols:]
    out_weight = out_weight.reshape(ring, width // 256, out_rows, 256).transpose(0, 2, 1, 3)
    out_weight = out_weight.reshape(ring * out_rows, width)

    gate_up_pieces = jnp.concatenate(
        [w_gate.reshape(gain_rows, TP, ff_cols), w_up.reshape(gain_rows, TP, ff_cols)], axis=2
    ).transpose(1, 0, 2)
    gate_up_item = lay.exchange(gate_up_pieces)
    gate_up_weight = lay.ring_gather(gate_up_item[:, None], 1).reshape(width, 2 * ff_cols)
    down_weight = lay.ring_gather(w_down[None], 0).reshape(ff_cols, width)

    packed = route(tokens)
    loss_rows, packed_held = lax.optimization_barrier(
        (jnp.concatenate([teacher, out_grad], axis=1), packed)
    )
    loss_rows = route(loss_rows)
    inputs = packed.astype(F32)
    group_rows = lay.gather_tokens(packed)
    group_rows, loss_rows = lax.optimization_barrier((group_rows, loss_rows))
    teacher_rows = loss_rows[:, :width]
    seed_rows = loss_rows[:, width:]
    group_lengths = jnp.stack([seq_lengths[(lay.t ^ k) * ring + lay.g] for k in (0, 2, 1, 3)])
    positions, allowed, valid_group = jax.vmap(lambda ls: segment_info(ls, rows))(group_lengths)
    valid_rows = valid_group[0].astype(F32)
    cosine, sine_table = rope_tables(positions.reshape(all_rows), HD)

    def prepare(q_raw, k_raw, q_scale, k_scale):
        query = norm_rows(q_raw.reshape(all_rows, heads, HD), q_scale)
        key_rows = norm_rows(k_raw, k_scale)
        query = rotate(query, cosine[:, None, :], sine_table[:, None, :])
        return (query, rotate(key_rows, cosine, sine_table))

    normed = norm_rows(group_rows.astype(F32), attn_gain_all).astype(BF16)
    qkv = dot(normed, qkv_weight)
    value_rows = qkv[:, q_cols + kv_cols :].astype(BF16).reshape(TP, rows, HD)
    (query_rot, key_rot), prepare_back = jax.vjp(
        prepare,
        qkv[:, :q_cols],
        qkv[:, q_cols : q_cols + kv_cols],
        query_gain.astype(F32),
        key_gain.astype(F32),
    )
    query_low = query_rot.astype(BF16).reshape(TP, rows, heads, HD)
    key_low = key_rot.astype(BF16).reshape(TP, rows, HD)
    scores = (
        jnp.einsum("brhd,bcd->bhrc", query_low, key_low, preferred_element_type=F32) * HD**-0.5
    )
    scores = jnp.where(allowed[:, None], scores, NEGATIVE)
    log_total = jax.nn.logsumexp(scores, axis=-1)
    prob_rows = jnp.exp(scores - log_total[..., None])
    prob_low = prob_rows.astype(BF16)
    heads_out = jnp.einsum("bhrc,bcd->brhd", prob_low, value_rows, preferred_element_type=F32)
    heads_out = heads_out.reshape(all_rows, q_cols).astype(BF16)
    hidden = inputs + lay.scatter_tokens(lambda part: dot(part, out_weight), heads_out)
    ffn_own, ffn_norm_back = jax.vjp(norm_rows, hidden, ffn_gain_all)
    ffn_in = lay.gather_tokens(ffn_own.astype(BF16))
    gate_up = dot(ffn_in, gate_up_weight)
    act_value, act_back = jax.vjp(swiglu, gate_up[:, :ff_cols], gate_up[:, ff_cols:])
    act_low = act_value.astype(BF16)
    result = hidden + lay.scatter_tokens(lambda part: dot(part, down_weight), act_low)
    result_low = result.astype(BF16)

    row_error = result_low.astype(F32) - teacher_rows.astype(F32)
    loss_part = jnp.sum(valid_rows * jnp.mean(row_error * row_error, axis=-1))
    upstream = seed_rows.astype(F32) + loss_ratio * valid_rows[:, None] * row_error
    upstream_low = lay.gather_tokens(upstream.astype(BF16))

    act_grad = dot_back(upstream_low, down_weight)
    down_grad = dot_rows(act_low, upstream_low).astype(BF16)
    gate_grad, up_grad = act_back(act_grad)
    gate_up_low = jnp.concatenate([gate_grad.astype(BF16), up_grad.astype(BF16)], axis=1)
    ffn_in_grad = lay.scatter_tokens(lambda part: dot_back(part, gate_up_weight), gate_up_low)
    hidden_part, ffn_gain_part = ffn_norm_back(ffn_in_grad)
    hidden_grad = upstream + hidden_part
    gate_up_grad = dot_rows(ffn_in, gate_up_low).astype(BF16)

    down_shard = lay.ring_scatter(down_grad.reshape(ring, ff_cols // ring, width), 0)[0]
    gate_up_sum = lay.ring_scatter(gate_up_grad.reshape(TP, ring, gain_rows, 2 * ff_cols), 1)

    hidden_low = lay.gather_tokens(hidden_grad.astype(BF16))
    out_w_grad = dot_rows(heads_out, hidden_low).astype(BF16)
    head_grad = dot_back(hidden_low, out_weight).astype(BF16).reshape(TP, rows, heads, HD)
    value_grad = jnp.einsum("bhrc,brhd->bcd", prob_low, head_grad, preferred_element_type=F32)
    prob_grad = jnp.einsum("brhd,bcd->bhrc", head_grad, value_rows, preferred_element_type=F32)
    score_grad = prob_rows * (prob_grad - jnp.sum(prob_rows * prob_grad, axis=-1, keepdims=True))
    score_low = score_grad.astype(BF16)
    query_grad = (
        jnp.einsum("bhrc,bcd->brhd", score_low, key_low, preferred_element_type=F32) * HD**-0.5
    )
    key_grad = (
        jnp.einsum("bhrc,brhd->bcd", score_low, query_low, preferred_element_type=F32) * HD**-0.5
    )
    q_raw_grad, k_raw_grad, q_gain_part, k_gain_part = prepare_back(
        (query_grad.reshape(all_rows, heads, HD), key_grad.reshape(all_rows, HD))
    )
    qkv_low = jnp.concatenate(
        [
            q_raw_grad.astype(BF16),
            k_raw_grad.astype(BF16),
            value_grad.astype(BF16).reshape(all_rows, HD),
        ],
        axis=1,
    )
    qkv_grad = dot_rows(normed, qkv_low).astype(BF16)

    attn_blocks = jnp.concatenate(
        [
            qkv_grad.reshape(TP, ring, gain_rows, qkv_cols)
            .transpose(1, 0, 2, 3)
            .reshape(ring, TP * gain_rows, qkv_cols),
            out_w_grad.reshape(ring, out_rows, width // 256, 256)
            .transpose(0, 2, 1, 3)
            .reshape(ring, out_rows * (width // 256), 256),
        ],
        axis=2,
    )
    attn_sum = lay.ring_scatter(attn_blocks, 0)[0]

    normed_grad = lay.scatter_tokens(lambda part: dot_back(part, qkv_weight), qkv_low)
    unused, attn_norm_back = jax.vjp(norm_rows, inputs, attn_gain_all)
    input_part, attn_gain_part = attn_norm_back(normed_grad)
    packed_grad = hidden_grad + input_part

    small = jnp.stack(
        [
            attn_gain_part,
            ffn_gain_part,
            jnp.concatenate(
                [
                    q_gain_part,
                    k_gain_part,
                    loss_part[None],
                    jnp.zeros((width - 2 * HD - 1,), F32),
                ]
            ),
        ]
    )
    small = jnp.pad(small, ((0, 5), (0, 0)))
    bit = 1
    while bit < devices:
        small = small + lay.flip(small, bit)
        bit = bit * 2
    attn_gain_shard = lax.dynamic_slice_in_dim(small[0], lay.me * gain_rows, gain_rows)
    ffn_gain_shard = lax.dynamic_slice_in_dim(small[1], lay.me * gain_rows, gain_rows)

    qkv_shard = lay.exchange(
        attn_sum[:, :qkv_cols].reshape(TP, gain_rows, qkv_cols).astype(BF16)
    ).astype(F32)
    gate_up_shard = lay.exchange(
        gate_up_sum.reshape(TP, gain_rows, 2 * ff_cols).astype(BF16)
    ).astype(F32)

    def whole(part):
        return part.transpose(1, 0, 2).reshape(gain_rows, -1)

    out_shard = (
        attn_sum[:, qkv_cols:].reshape(width // 256, out_rows, 256).transpose(1, 0, 2)
    ).reshape(out_rows, width)
    returned = route_back(jnp.concatenate([result_low, packed_grad.astype(BF16)], axis=1))
    return (
        returned[:, :width].astype(BF16),
        small[2, 2 * HD] / valid_count,
        returned[:, width:],
        attn_gain_shard,
        whole(qkv_shard[:, :, :q_cols]),
        whole(qkv_shard[:, :, q_cols : q_cols + kv_cols]),
        whole(qkv_shard[:, :, q_cols + kv_cols :]),
        out_shard,
        small[2, :HD],
        small[2, HD : 2 * HD],
        ffn_gain_shard,
        whole(gate_up_shard[:, :, :ff_cols]),
        whole(gate_up_shard[:, :, ff_cols:]),
        down_shard,
    )


def solution(mesh):
    rows = P(AXES, None)
    flat = P(AXES)
    in_specs = (rows, rows, rows, flat, rows, rows, rows, rows, P(), P(), flat)
    in_specs = in_specs + (rows, rows, rows, P(), rows, rows)
    out_specs = (rows, P(), rows, flat, rows, rows, rows, rows, P(), P(), flat, rows, rows, rows)
    return jax.shard_map(shards, mesh=mesh, in_specs=in_specs, out_specs=out_specs, check_vma=False)
```

```python
import jax
import jax.numpy as jnp
from jax import lax
from jax.sharding import PartitionSpec as P

KV_HEADS = 4
HD = 64
TP = 4
AXES = ("dp", "fsdp")

EPS = 1e-06
THETA = 10000.0
NEGATIVE = -1000000000.0

BF16 = jnp.bfloat16
F32 = jnp.float32


def segment_info(lengths, row_count):
    seq_ends = jnp.cumsum(lengths)
    seq_starts = seq_ends - lengths
    row_index = jnp.arange(row_count, dtype=jnp.int32)
    segment = jnp.sum((row_index[:, None] >= seq_ends[None, :]).astype(jnp.int32), axis=1)
    seg_first = jnp.concatenate([seq_starts, seq_ends[-1:]])
    labels = jnp.arange(seg_first.shape[0], dtype=jnp.int32)
    seg_begin = jnp.sum(
        jnp.where(segment[:, None] == labels[None, :], seg_first[None, :], 0), axis=1
    )
    allowed = (segment[:, None] == segment[None, :]) & (row_index[None, :] <= row_index[:, None])
    return (row_index - seg_begin, allowed, segment < lengths.shape[0])


def norm_rows(values, gain_vec):
    return values * lax.rsqrt(jnp.mean(values * values, axis=-1, keepdims=True) + EPS) * gain_vec


def rope_tables(positions, head_width):
    half_width = head_width // 2
    frequency = THETA ** (-(jnp.arange(half_width, dtype=F32) * 2.0) / head_width)
    angles = positions.astype(F32)[:, None] * frequency[None, :]
    return (jnp.cos(angles), jnp.sin(angles))


def rotate(values, cosine, sine_table):
    half_width = values.shape[-1] // 2
    front_half = values[..., :half_width]
    second = values[..., half_width:]
    return jnp.concatenate(
        [front_half * cosine - second * sine_table, front_half * sine_table + second * cosine],
        axis=-1,
    )


def swiglu(gate_rows, up_rows):
    return jax.nn.silu(gate_rows) * up_rows


def dot(left, right):
    return jnp.dot(left, right, preferred_element_type=F32)


def dot_rows(left, right):
    return jnp.einsum("ra,rb->ab", left, right, preferred_element_type=F32)


def dot_back(left, right):
    return jnp.einsum("ra,ba->rb", left, right, preferred_element_type=F32)


def tie(*values):
    return lax.optimization_barrier(values)


class Layout:
    def __init__(self, devices):
        self.devices = devices
        self.ring = devices // TP
        evens = list(range(0, self.ring, 2))
        odds = list(range(1, self.ring, 2))
        self.cycle = evens + odds[::-1]
        self.place = [self.cycle.index(g) for g in range(self.ring)]
        self.me = lax.axis_index("dp") * lax.axis_size("fsdp") + lax.axis_index("fsdp")
        self.t = self.me // self.ring
        self.g = self.me % self.ring
        half = self.g // 2
        self.pos = jnp.where(self.g == 2 * half, half, self.ring - 1 - half)

    def at(self, distance):
        index = self.pos + (distance % self.ring)
        index = jnp.where(index < self.ring, index, index - self.ring)
        return jnp.minimum(2 * index, 2 * self.ring - 1 - 2 * index)

    def swap(self, value, bit):
        pairs = [
            (t * self.ring + g, (t ^ bit) * self.ring + g)
            for t in range(TP)
            for g in range(self.ring)
        ]
        return lax.ppermute(value, AXES, pairs)

    def shift(self, value, step):
        pairs = [
            (t * self.ring + g, t * self.ring + self.cycle[(self.place[g] + step) % self.ring])
            for t in range(TP)
            for g in range(self.ring)
        ]
        return lax.ppermute(value, AXES, pairs)

    def flip(self, value, bit):
        return lax.ppermute(value, AXES, [(n, n ^ bit) for n in range(self.devices)])

    def gather_tokens(self, own):
        across = self.swap(own, 2)
        core = self.swap(own, 1)
        far = self.swap(across, 1)
        return jnp.concatenate([own, across, core, far], axis=0)

    def scatter_near(self, product, rows):
        half = rows.shape[0] // 2
        own = half // 2
        sent = product(rows[half:]).astype(BF16)
        kept = product(rows[:half]) + self.swap(sent, 1).astype(F32)
        return kept[:own], kept[own:].astype(BF16)

    def scatter_tokens(self, product, rows):
        kept, sent = self.scatter_near(product, rows)
        return kept + self.swap(sent, 2).astype(F32)

    def exchange(self, pieces):
        got = []
        for bit in range(TP):
            piece = lax.dynamic_index_in_dim(pieces, self.t ^ bit, 0, keepdims=False)
            got.append(self.swap(piece, bit) if bit else piece)
        for bit in (1, 2):
            turned = (self.t & bit) != 0
            got = [jnp.where(turned, got[k ^ bit], got[k]) for k in range(TP)]
        return got

    def ring_gather(self, items, axes, hook=None):
        count = len(items)
        fulls = []
        for item, axis in zip(items, axes):
            shape = list(item.shape)
            shape[axis] = self.ring
            full = jnp.zeros(tuple(shape), item.dtype)
            fulls.append(lax.dynamic_update_slice_in_dim(full, item, self.g, axis))
        rights = list(items)
        lefts = list(items)
        last = self.ring // 2
        for step in range(1, last):
            for k in range(count):
                rights[k] = self.shift(rights[k], 1)
                lefts[k] = self.shift(lefts[k], -1)
            if hook is not None:
                moving = hook(step, rights + lefts)
                rights = list(moving[:count])
                lefts = list(moving[count:])
            for k in range(count):
                fulls[k] = lax.dynamic_update_slice_in_dim(
                    fulls[k], rights[k], self.at(-step), axes[k]
                )
                fulls[k] = lax.dynamic_update_slice_in_dim(
                    fulls[k], lefts[k], self.at(step), axes[k]
                )
        for k in range(count):
            item = items[k]
            split = 0 if axes[k] else 1
            half = item.shape[split] // 2
            first = self.shift(lax.slice_in_dim(rights[k], 0, half, axis=split), 1)
            second = self.shift(lax.slice_in_dim(lefts[k], half, 2 * half, axis=split), -1)
            start = [jnp.int32(0)] * item.ndim
            start[axes[k]] = self.at(last)
            full = lax.dynamic_update_slice(fulls[k], first, start)
            start[split] = jnp.int32(half)
            fulls[k] = lax.dynamic_update_slice(full, second, start)
        return fulls

    def ring_scatter(self, full, axis, hook=tie):
        last = self.ring // 2

        def block(distance):
            return lax.dynamic_slice_in_dim(full, self.at(distance), 1, axis)

        split = 0 if axis else 1
        edge = block(last)
        half = edge.shape[split] // 2
        right = self.shift(lax.slice_in_dim(edge, 0, half, axis=split), 1)
        left = self.shift(lax.slice_in_dim(edge, half, 2 * half, axis=split), -1)
        pad = [(0, 0, 0)] * edge.ndim
        pad[split] = (0, half, 0)
        right = lax.pad(right, jnp.zeros((), BF16), pad)
        pad[split] = (half, 0, 0)
        left = lax.pad(left, jnp.zeros((), BF16), pad)
        for step in range(last - 1, 0, -1):
            right = (block(step).astype(F32) + right.astype(F32)).astype(BF16)
            left = (block(-step).astype(F32) + left.astype(F32)).astype(BF16)
            right, left = hook(right, left)
            right = self.shift(right, 1)
            left = self.shift(left, -1)
        return block(0).astype(F32) + right.astype(F32) + left.astype(F32)


def shards(
    tokens,
    teacher,
    out_grad,
    attn_gain,
    w_query,
    w_key,
    w_value,
    w_out,
    query_gain,
    key_gain,
    ffn_gain,
    w_gate,
    w_up,
    w_down,
    seq_lengths,
    send_order,
    pack_order,
):
    groups = lax.axis_size("fsdp")
    devices = lax.axis_size("dp") * groups
    lay = Layout(devices)
    ring = lay.ring
    rows = tokens.shape[0]
    width = tokens.shape[1]
    gain_rows = attn_gain.shape[0]
    q_cols = w_query.shape[1] // TP
    kv_cols = w_key.shape[1] // TP
    qkv_cols = q_cols + 2 * kv_cols
    heads = q_cols // HD
    ff_cols = w_gate.shape[1] // TP
    out_rows = w_out.shape[0]
    all_rows = TP * rows

    my_lengths = seq_lengths[lay.me]
    valid_count = jnp.sum(seq_lengths).astype(F32)
    loss_ratio = float(devices * rows) / valid_count
    send_rows = send_order[0]
    pack_rows = pack_order[0]
    counting = jnp.arange(rows, dtype=jnp.int32)
    send_pick = (send_rows[:, None] == counting[None, :]).astype(BF16)
    pack_pick = (pack_rows[:, None] == counting[None, :]).astype(BF16)

    def to_all(values):
        return lax.all_to_all(values, "fsdp", split_axis=0, concat_axis=0, tiled=True)

    def route(values):
        sent = to_all(dot(send_pick, values).astype(BF16))
        return dot(pack_pick, sent).astype(BF16)

    def route_back(values):
        sent = to_all(dot_rows(pack_pick, values).astype(BF16))
        return dot_rows(send_pick, sent)

    pad_rows = 8
    qkv_pieces = jnp.concatenate(
        [
            w_query.reshape(gain_rows, TP, q_cols),
            w_key.reshape(gain_rows, TP, kv_cols),
            w_value.reshape(gain_rows, TP, kv_cols),
        ],
        axis=2,
    ).transpose(1, 0, 2)
    gain_line = jnp.concatenate(
        [
            jnp.pad(attn_gain, (0, 128 - gain_rows)),
            jnp.pad(ffn_gain, (0, 128 - gain_rows)),
            jnp.zeros((qkv_cols - 256,), BF16),
        ]
    )
    gain_block = jnp.broadcast_to(gain_line[None, None], (TP, pad_rows, qkv_cols))
    qkv_item = jnp.concatenate(
        lay.exchange(jnp.concatenate([qkv_pieces, gain_block], axis=1)), axis=0
    )
    item_rows = TP * (gain_rows + pad_rows)
    out_item = w_out.reshape(out_rows, width // 256, 256).transpose(1, 0, 2)
    out_item = out_item.reshape(out_rows * (width // 256), 256)
    out_item = jnp.pad(out_item, ((0, item_rows - out_item.shape[0]), (0, 0)))
    attn_item = jnp.concatenate([qkv_item, out_item], axis=1)
    (attn_full,) = lay.ring_gather([attn_item[None]], [0])
    qkv_full = attn_full[:, :, :qkv_cols].reshape(ring, TP, gain_rows + pad_rows, qkv_cols)
    qkv_weight = qkv_full[:, :, :gain_rows].transpose(1, 0, 2, 3).reshape(width, qkv_cols)
    gain_full = qkv_full[:, :, gain_rows].transpose(1, 0, 2)
    attn_gain_all = gain_full[:, :, :gain_rows].reshape(width).astype(F32)
    ffn_gain_all = gain_full[:, :, 128 : 128 + gain_rows].reshape(width).astype(F32)
    out_weight = attn_full[:, : out_rows * (width // 256), qkv_cols:]
    out_weight = out_weight.reshape(ring, width // 256, out_rows, 256).transpose(0, 2, 1, 3)
    out_weight = out_weight.reshape(ring * out_rows, width)

    gate_up_pieces = jnp.concatenate(
        [w_gate.reshape(gain_rows, TP, ff_cols), w_up.reshape(gain_rows, TP, ff_cols)], axis=2
    ).transpose(1, 0, 2)
    gate_up_item = jnp.stack(lay.exchange(gate_up_pieces))
    down_item = w_down
    gate_up_full, down_full = lay.ring_gather(
        [gate_up_item[:, None], down_item[None]], [1, 0]
    )
    gate_up_weight = gate_up_full.reshape(width, 2 * ff_cols)
    down_weight = down_full.reshape(ff_cols, width)

    packed = route(tokens)
    loss_rows = route(jnp.concatenate([teacher, out_grad], axis=1))
    inputs = packed.astype(F32)
    group_rows = lay.gather_tokens(packed)
    teacher_rows = loss_rows[:, :width]
    seed_rows = loss_rows[:, width:]
    group_lengths = jnp.stack([seq_lengths[(lay.t ^ k) * ring + lay.g] for k in (0, 2, 1, 3)])
    positions, allowed, valid_group = jax.vmap(lambda ls: segment_info(ls, rows))(group_lengths)
    valid_rows = valid_group[0].astype(F32)
    cosine, sine_table = rope_tables(positions.reshape(all_rows), HD)

    def prepare(q_raw, k_raw, q_scale, k_scale):
        query = norm_rows(q_raw.reshape(all_rows, heads, HD), q_scale)
        key_rows = norm_rows(k_raw, k_scale)
        query = rotate(query, cosine[:, None, :], sine_table[:, None, :])
        return (query, rotate(key_rows, cosine, sine_table))

    normed = norm_rows(group_rows.astype(F32), attn_gain_all).astype(BF16)
    qkv = dot(normed, qkv_weight)
    value_rows = qkv[:, q_cols + kv_cols :].astype(BF16).reshape(TP, rows, HD)
    (query_rot, key_rot), prepare_back = jax.vjp(
        prepare,
        qkv[:, :q_cols],
        qkv[:, q_cols : q_cols + kv_cols],
        query_gain.astype(F32),
        key_gain.astype(F32),
    )
    query_low = query_rot.astype(BF16).reshape(TP, rows, heads, HD)
    key_low = key_rot.astype(BF16).reshape(TP, rows, HD)
    scores = (
        jnp.einsum("brhd,bcd->bhrc", query_low, key_low, preferred_element_type=F32) * HD**-0.5
    )
    scores = jnp.where(allowed[:, None], scores, NEGATIVE)
    log_total = jax.nn.logsumexp(scores, axis=-1)
    prob_rows = jnp.exp(scores - log_total[..., None])
    prob_low = prob_rows.astype(BF16)
    heads_out = jnp.einsum("bhrc,bcd->brhd", prob_low, value_rows, preferred_element_type=F32)
    heads_out = heads_out.reshape(all_rows, q_cols).astype(BF16)
    hidden = inputs + lay.scatter_tokens(lambda part: dot(part, out_weight), heads_out)
    ffn_own, ffn_norm_back = jax.vjp(lambda v: norm_rows(v, ffn_gain_all), hidden)
    ffn_in = lay.gather_tokens(ffn_own.astype(BF16))
    gate_up = dot(ffn_in, gate_up_weight)
    act_value, act_back = jax.vjp(swiglu, gate_up[:, :ff_cols], gate_up[:, ff_cols:])
    act_low = act_value.astype(BF16)
    result = hidden + lay.scatter_tokens(lambda part: dot(part, down_weight), act_low)
    result_low = result.astype(BF16)

    row_error = result_low.astype(F32) - teacher_rows.astype(F32)
    loss_part = jnp.sum(valid_rows * jnp.mean(row_error * row_error, axis=-1))
    upstream = seed_rows.astype(F32) + loss_ratio * valid_rows[:, None] * row_error
    upstream_own = upstream.astype(BF16)
    upstream_low = lay.gather_tokens(upstream_own)
    mixed = route_back(result_low).astype(BF16)

    act_grad = dot_back(upstream_low, down_weight)
    down_grad = dot_rows(act_low, upstream_low).astype(BF16)
    gate_grad, up_grad = act_back(act_grad)
    gate_up_low = jnp.concatenate([gate_grad.astype(BF16), up_grad.astype(BF16)], axis=1)
    ffn_in_grad = lay.scatter_tokens(lambda part: dot_back(part, gate_up_weight), gate_up_low)
    (hidden_part,) = ffn_norm_back(ffn_in_grad)
    hidden_grad = upstream + hidden_part
    hidden_own = hidden_grad.astype(BF16)
    gate_up_grad = dot_rows(ffn_in, gate_up_low).astype(BF16)

    hidden_low = lay.gather_tokens(hidden_own)
    out_w_grad = dot_rows(heads_out, hidden_low).astype(BF16)
    head_grad = dot_back(hidden_low, out_weight).astype(BF16).reshape(TP, rows, heads, HD)
    value_grad = jnp.einsum("bhrc,brhd->bcd", prob_low, head_grad, preferred_element_type=F32)
    prob_grad = jnp.einsum("brhd,bcd->bhrc", head_grad, value_rows, preferred_element_type=F32)
    score_grad = prob_rows * (prob_grad - jnp.sum(prob_rows * prob_grad, axis=-1, keepdims=True))
    score_low = score_grad.astype(BF16)
    query_grad = (
        jnp.einsum("bhrc,bcd->brhd", score_low, key_low, preferred_element_type=F32) * HD**-0.5
    )
    key_grad = (
        jnp.einsum("bhrc,brhd->bcd", score_low, query_low, preferred_element_type=F32) * HD**-0.5
    )
    q_raw_grad, k_raw_grad, q_gain_part, k_gain_part = prepare_back(
        (query_grad.reshape(all_rows, heads, HD), key_grad.reshape(all_rows, HD))
    )
    qkv_low = jnp.concatenate(
        [
            q_raw_grad.astype(BF16),
            k_raw_grad.astype(BF16),
            value_grad.astype(BF16).reshape(all_rows, HD),
        ],
        axis=1,
    )
    qkv_grad = dot_rows(normed, qkv_low).astype(BF16)

    down_shard = lay.ring_scatter(down_grad.reshape(ring, ff_cols // ring, width), 0)[0]
    gate_up_sum = lay.ring_scatter(gate_up_grad.reshape(TP, ring, gain_rows, 2 * ff_cols), 1)

    attn_blocks = jnp.concatenate(
        [
            qkv_grad.reshape(TP, ring, gain_rows, qkv_cols)
            .transpose(1, 0, 2, 3)
            .reshape(ring, TP * gain_rows, qkv_cols),
            out_w_grad.reshape(ring, out_rows, width // 256, 256)
            .transpose(0, 2, 1, 3)
            .reshape(ring, out_rows * (width // 256), 256),
        ],
        axis=2,
    )
    attn_sum = lay.ring_scatter(attn_blocks, 0)[0]

    normed_grad = lay.scatter_tokens(lambda part: dot_back(part, qkv_weight), qkv_low)
    unused, attn_norm_back = jax.vjp(lambda v: norm_rows(v, attn_gain_all), inputs)
    packed_grad = hidden_grad + attn_norm_back(normed_grad)[0]

    small = jnp.concatenate(
        [q_gain_part, k_gain_part, loss_part[None], jnp.zeros((128 - 1,), F32)]
    )[None]
    bit = 1
    while bit < devices:
        small = small + lay.flip(small, bit)
        bit = bit * 2
    small = small[0]

    qkv_parts = lay.exchange(
        attn_sum[:, :qkv_cols].reshape(TP, gain_rows, qkv_cols).astype(BF16)
    )
    gate_up_parts = lay.exchange(
        gate_up_sum.reshape(TP, gain_rows, 2 * ff_cols).astype(BF16)
    )

    def whole(parts, first, last):
        return jnp.concatenate([part[:, first:last] for part in parts], axis=1).astype(F32)

    query_grad_shard = whole(qkv_parts, 0, q_cols)
    key_grad_shard = whole(qkv_parts, q_cols, q_cols + kv_cols)
    value_grad_shard = whole(qkv_parts, q_cols + kv_cols, qkv_cols)
    gate_grad_shard = whole(gate_up_parts, 0, ff_cols)
    up_grad_shard = whole(gate_up_parts, ff_cols, 2 * ff_cols)

    def gain_grad(gain, *pairs):
        total = 0.0
        for weight, grad in pairs:
            total = total + jnp.sum(weight.astype(F32) * grad, axis=1)
        return total / gain.astype(F32)

    attn_gain_shard = gain_grad(
        attn_gain,
        (w_query, query_grad_shard),
        (w_key, key_grad_shard),
        (w_value, value_grad_shard),
    )
    ffn_gain_shard = gain_grad(ffn_gain, (w_gate, gate_grad_shard), (w_up, up_grad_shard))
    out_shard = (
        attn_sum[:, qkv_cols:].reshape(width // 256, out_rows, 256).transpose(1, 0, 2)
    ).reshape(out_rows, width)
    return (
        mixed,
        small[2 * HD] / valid_count,
        route_back(packed_grad.astype(BF16)),
        attn_gain_shard,
        query_grad_shard,
        key_grad_shard,
        value_grad_shard,
        out_shard,
        small[:HD],
        small[HD : 2 * HD],
        ffn_gain_shard,
        gate_grad_shard,
        up_grad_shard,
        down_shard,
    )


def solution(mesh):
    rows = P(AXES, None)
    flat = P(AXES)
    in_specs = (rows, rows, rows, flat, rows, rows, rows, rows, P(), P(), flat)
    in_specs = in_specs + (rows, rows, rows, P(), rows, rows)
    out_specs = (rows, P(), rows, flat, rows, rows, rows, rows, P(), P(), flat, rows, rows, rows)
    return jax.shard_map(shards, mesh=mesh, in_specs=in_specs, out_specs=out_specs, check_vma=False)
```

```python
import jax
import jax.numpy as jnp
from jax import lax
from jax.sharding import PartitionSpec as P

KV_HEADS = 4
HD = 64
TP = 4
AXES = ("dp", "fsdp")

EPS = 1e-06
THETA = 10000.0
NEGATIVE = -1000000000.0

BF16 = jnp.bfloat16
F32 = jnp.float32


def segment_info(lengths, row_count):
    seq_ends = jnp.cumsum(lengths)
    seq_starts = seq_ends - lengths
    row_index = jnp.arange(row_count, dtype=jnp.int32)
    segment = jnp.sum((row_index[:, None] >= seq_ends[None, :]).astype(jnp.int32), axis=1)
    seg_first = jnp.concatenate([seq_starts, seq_ends[-1:]])
    labels = jnp.arange(seg_first.shape[0], dtype=jnp.int32)
    seg_begin = jnp.sum(
        jnp.where(segment[:, None] == labels[None, :], seg_first[None, :], 0), axis=1
    )
    allowed = (segment[:, None] == segment[None, :]) & (row_index[None, :] <= row_index[:, None])
    return (row_index - seg_begin, allowed, segment < lengths.shape[0])


def norm_rows(values, gain_vec):
    return values * lax.rsqrt(jnp.mean(values * values, axis=-1, keepdims=True) + EPS) * gain_vec


def rope_tables(positions, head_width):
    half_width = head_width // 2
    frequency = THETA ** (-(jnp.arange(half_width, dtype=F32) * 2.0) / head_width)
    angles = positions.astype(F32)[:, None] * frequency[None, :]
    return (jnp.cos(angles), jnp.sin(angles))


def rotate(values, cosine, sine_table):
    half_width = values.shape[-1] // 2
    front_half = values[..., :half_width]
    second = values[..., half_width:]
    return jnp.concatenate(
        [front_half * cosine - second * sine_table, front_half * sine_table + second * cosine],
        axis=-1,
    )


def swiglu(gate_rows, up_rows):
    return jax.nn.silu(gate_rows) * up_rows


def dot(left, right):
    return jnp.dot(left, right, preferred_element_type=F32)


def dot_rows(left, right):
    return jnp.einsum("ra,rb->ab", left, right, preferred_element_type=F32)


def dot_back(left, right):
    return jnp.einsum("ra,ba->rb", left, right, preferred_element_type=F32)


def after(value, *others):
    return lax.optimization_barrier((value,) + others)[0]


class Layout:
    def __init__(self, devices):
        self.devices = devices
        self.ring = devices // TP
        evens = list(range(0, self.ring, 2))
        odds = list(range(1, self.ring, 2))
        self.cycle = evens + odds[::-1]
        self.place = [self.cycle.index(g) for g in range(self.ring)]
        self.me = lax.axis_index("dp") * lax.axis_size("fsdp") + lax.axis_index("fsdp")
        self.t = self.me // self.ring
        self.g = self.me % self.ring
        half = self.g // 2
        self.pos = jnp.where(self.g == 2 * half, half, self.ring - 1 - half)

    def at(self, distance):
        index = self.pos + (distance % self.ring)
        index = jnp.where(index < self.ring, index, index - self.ring)
        return jnp.minimum(2 * index, 2 * self.ring - 1 - 2 * index)

    def swap(self, value, bit):
        pairs = [
            (t * self.ring + g, (t ^ bit) * self.ring + g)
            for t in range(TP)
            for g in range(self.ring)
        ]
        return lax.ppermute(value, AXES, pairs)

    def shift(self, value, step):
        pairs = [
            (t * self.ring + g, t * self.ring + self.cycle[(self.place[g] + step) % self.ring])
            for t in range(TP)
            for g in range(self.ring)
        ]
        return lax.ppermute(value, AXES, pairs)

    def flip(self, value, bit):
        return lax.ppermute(value, AXES, [(n, n ^ bit) for n in range(self.devices)])

    def gather_tokens(self, own):
        across = self.swap(own, 2)
        core = self.swap(own, 1)
        far = self.swap(across, 1)
        return jnp.concatenate([own, across, core, far], axis=0)

    def scatter_tokens(self, product, rows):
        half = rows.shape[0] // 2
        own = half // 2
        sent = product(rows[half:]).astype(BF16)
        kept = product(rows[:half]) + self.swap(sent, 1).astype(F32)
        far = kept[own:].astype(BF16)
        return kept[:own] + self.swap(far, 2).astype(F32), far

    def exchange(self, pieces):
        got = []
        for bit in range(TP):
            piece = lax.dynamic_index_in_dim(pieces, self.t ^ bit, 0, keepdims=False)
            got.append(self.swap(piece, bit) if bit else piece)
        for bit in (1, 2):
            turned = (self.t & bit) != 0
            got = [jnp.where(turned, got[k ^ bit], got[k]) for k in range(TP)]
        return got

    def ring_gather(self, items, axes):
        count = len(items)
        fulls = []
        for item, axis in zip(items, axes):
            shape = list(item.shape)
            shape[axis] = self.ring
            full = jnp.zeros(tuple(shape), item.dtype)
            fulls.append(lax.dynamic_update_slice_in_dim(full, item, self.g, axis))
        rights = list(items)
        lefts = list(items)
        last = self.ring // 2
        for step in range(1, last):
            for k in range(count):
                rights[k] = self.shift(rights[k], 1)
                lefts[k] = self.shift(lefts[k], -1)
            for k in range(count):
                fulls[k] = lax.dynamic_update_slice_in_dim(
                    fulls[k], rights[k], self.at(-step), axes[k]
                )
                fulls[k] = lax.dynamic_update_slice_in_dim(
                    fulls[k], lefts[k], self.at(step), axes[k]
                )
        for k in range(count):
            item = items[k]
            split = 0 if axes[k] else 1
            half = item.shape[split] // 2
            first = self.shift(lax.slice_in_dim(rights[k], 0, half, axis=split), 1)
            second = self.shift(lax.slice_in_dim(lefts[k], half, 2 * half, axis=split), -1)
            start = [jnp.int32(0)] * item.ndim
            start[axes[k]] = self.at(last)
            full = lax.dynamic_update_slice(fulls[k], first, start)
            start[split] = jnp.int32(half)
            fulls[k] = lax.dynamic_update_slice(full, second, start)
        return fulls, tuple(rights) + tuple(lefts)

    def ring_scatter(self, full, axis, gates):
        last = self.ring // 2

        def block(distance):
            index = self.at(distance)
            gate = gates[abs(distance)] if abs(distance) < len(gates) else None
            if gate is not None:
                index = after(index, gate)
            return lax.dynamic_slice_in_dim(full, index, 1, axis)

        split = 0 if axis else 1
        edge = block(last)
        half = edge.shape[split] // 2
        right = self.shift(lax.slice_in_dim(edge, 0, half, axis=split), 1)
        left = self.shift(lax.slice_in_dim(edge, half, 2 * half, axis=split), -1)
        pad = [(0, 0, 0)] * edge.ndim
        pad[split] = (0, half, 0)
        right = lax.pad(right, jnp.zeros((), BF16), pad)
        pad[split] = (half, 0, 0)
        left = lax.pad(left, jnp.zeros((), BF16), pad)
        for step in range(last - 1, 0, -1):
            right = (block(step).astype(F32) + right.astype(F32)).astype(BF16)
            left = (block(-step).astype(F32) + left.astype(F32)).astype(BF16)
            right, left = lax.optimization_barrier((right, left))
            right = self.shift(right, 1)
            left = self.shift(left, -1)
        return block(0).astype(F32) + right.astype(F32) + left.astype(F32)


def shards(
    tokens,
    teacher,
    out_grad,
    attn_gain,
    w_query,
    w_key,
    w_value,
    w_out,
    query_gain,
    key_gain,
    ffn_gain,
    w_gate,
    w_up,
    w_down,
    seq_lengths,
    send_order,
    pack_order,
):
    groups = lax.axis_size("fsdp")
    devices = lax.axis_size("dp") * groups
    lay = Layout(devices)
    ring = lay.ring
    rows = tokens.shape[0]
    width = tokens.shape[1]
    gain_rows = attn_gain.shape[0]
    q_cols = w_query.shape[1] // TP
    kv_cols = w_key.shape[1] // TP
    qkv_cols = q_cols + 2 * kv_cols
    heads = q_cols // HD
    ff_cols = w_gate.shape[1] // TP
    out_rows = w_out.shape[0]
    all_rows = TP * rows

    my_lengths = seq_lengths[lay.me]
    valid_count = jnp.sum(seq_lengths).astype(F32)
    loss_ratio = float(devices * rows) / valid_count
    send_rows = send_order[0]
    pack_rows = pack_order[0]
    counting = jnp.arange(rows, dtype=jnp.int32)
    send_pick = (send_rows[:, None] == counting[None, :]).astype(BF16)
    pack_pick = (pack_rows[:, None] == counting[None, :]).astype(BF16)

    def to_all(values):
        return lax.all_to_all(values, "fsdp", split_axis=0, concat_axis=0, tiled=True)

    def route(values):
        sent = to_all(dot(send_pick, values).astype(BF16))
        return dot(pack_pick, sent).astype(BF16)

    def route_back(values):
        sent = to_all(dot_rows(pack_pick, values).astype(BF16))
        return dot_rows(send_pick, sent)

    pad_rows = 8
    qkv_pieces = jnp.concatenate(
        [
            w_query.reshape(gain_rows, TP, q_cols),
            w_key.reshape(gain_rows, TP, kv_cols),
            w_value.reshape(gain_rows, TP, kv_cols),
        ],
        axis=2,
    ).transpose(1, 0, 2)
    gain_line = jnp.concatenate(
        [
            jnp.pad(attn_gain, (0, 128 - gain_rows)),
            jnp.pad(ffn_gain, (0, 128 - gain_rows)),
            jnp.zeros((qkv_cols - 256,), BF16),
        ]
    )
    gain_block = jnp.broadcast_to(gain_line[None, None], (TP, pad_rows, qkv_cols))
    qkv_item = jnp.concatenate(
        lay.exchange(jnp.concatenate([qkv_pieces, gain_block], axis=1)), axis=0
    )
    item_rows = TP * (gain_rows + pad_rows)
    out_item = w_out.reshape(out_rows, width // 256, 256).transpose(1, 0, 2)
    out_item = out_item.reshape(out_rows * (width // 256), 256)
    out_item = jnp.pad(out_item, ((0, item_rows - out_item.shape[0]), (0, 0)))
    attn_item = jnp.concatenate([qkv_item, out_item], axis=1)
    (attn_full,), attn_sent = lay.ring_gather([attn_item[None]], [0])
    qkv_full = attn_full[:, :, :qkv_cols].reshape(ring, TP, gain_rows + pad_rows, qkv_cols)
    qkv_weight = qkv_full[:, :, :gain_rows].transpose(1, 0, 2, 3).reshape(width, qkv_cols)
    gain_full = qkv_full[:, :, gain_rows].transpose(1, 0, 2)
    attn_gain_all = gain_full[:, :, :gain_rows].reshape(width).astype(F32)
    ffn_gain_all = gain_full[:, :, 128 : 128 + gain_rows].reshape(width).astype(F32)
    out_weight = attn_full[:, : out_rows * (width // 256), qkv_cols:]
    out_weight = out_weight.reshape(ring, width // 256, out_rows, 256).transpose(0, 2, 1, 3)
    out_weight = out_weight.reshape(ring * out_rows, width)

    gate_up_pieces = jnp.concatenate(
        [w_gate.reshape(gain_rows, TP, ff_cols), w_up.reshape(gain_rows, TP, ff_cols)], axis=2
    ).transpose(1, 0, 2)
    gate_up_item = jnp.stack(lay.exchange(after(gate_up_pieces, qkv_item)))
    gate_up_item, down_item = lax.optimization_barrier((gate_up_item, w_down) + attn_sent)[:2]
    (gate_up_full, down_full), ffn_sent = lay.ring_gather(
        [gate_up_item[:, None], down_item[None]], [1, 0]
    )
    gate_up_weight = gate_up_full.reshape(width, 2 * ff_cols)
    down_weight = down_full.reshape(ff_cols, width)

    packed = route(tokens)
    loss_rows = route(after(jnp.concatenate([teacher, out_grad], axis=1), *ffn_sent))
    inputs = packed.astype(F32)
    group_rows = lay.gather_tokens(packed)
    teacher_rows = loss_rows[:, :width]
    seed_rows = loss_rows[:, width:]
    group_lengths = jnp.stack([seq_lengths[(lay.t ^ k) * ring + lay.g] for k in (0, 2, 1, 3)])
    positions, allowed, valid_group = jax.vmap(lambda ls: segment_info(ls, rows))(group_lengths)
    valid_rows = valid_group[0].astype(F32)
    cosine, sine_table = rope_tables(positions.reshape(all_rows), HD)

    def prepare(q_raw, k_raw, q_scale, k_scale):
        query = norm_rows(q_raw.reshape(all_rows, heads, HD), q_scale)
        key_rows = norm_rows(k_raw, k_scale)
        query = rotate(query, cosine[:, None, :], sine_table[:, None, :])
        return (query, rotate(key_rows, cosine, sine_table))

    normed = norm_rows(group_rows.astype(F32), attn_gain_all).astype(BF16)
    qkv = dot(normed, qkv_weight)
    value_rows = qkv[:, q_cols + kv_cols :].astype(BF16).reshape(TP, rows, HD)
    (query_rot, key_rot), prepare_back = jax.vjp(
        prepare,
        qkv[:, :q_cols],
        qkv[:, q_cols : q_cols + kv_cols],
        query_gain.astype(F32),
        key_gain.astype(F32),
    )
    query_low = query_rot.astype(BF16).reshape(TP, rows, heads, HD)
    key_low = key_rot.astype(BF16).reshape(TP, rows, HD)
    scores = (
        jnp.einsum("brhd,bcd->bhrc", query_low, key_low, preferred_element_type=F32) * HD**-0.5
    )
    scores = jnp.where(allowed[:, None], scores, NEGATIVE)
    log_total = jax.nn.logsumexp(scores, axis=-1)
    prob_rows = jnp.exp(scores - log_total[..., None])
    prob_low = prob_rows.astype(BF16)
    heads_out = jnp.einsum("bhrc,bcd->brhd", prob_low, value_rows, preferred_element_type=F32)
    heads_out = heads_out.reshape(all_rows, q_cols).astype(BF16)
    hidden_sum, unused_sent = lay.scatter_tokens(lambda part: dot(part, out_weight), heads_out)
    hidden = inputs + hidden_sum
    ffn_own, ffn_norm_back = jax.vjp(lambda v: norm_rows(v, ffn_gain_all), hidden)
    ffn_in = lay.gather_tokens(ffn_own.astype(BF16))
    gate_up = dot(ffn_in, gate_up_weight)
    act_value, act_back = jax.vjp(swiglu, gate_up[:, :ff_cols], gate_up[:, ff_cols:])
    act_low = act_value.astype(BF16)
    result_sum, unused_sent = lay.scatter_tokens(lambda part: dot(part, down_weight), act_low)
    result = hidden + result_sum
    result_low = result.astype(BF16)

    row_error = result_low.astype(F32) - teacher_rows.astype(F32)
    loss_part = jnp.sum(valid_rows * jnp.mean(row_error * row_error, axis=-1))
    upstream = seed_rows.astype(F32) + loss_ratio * valid_rows[:, None] * row_error
    upstream_own = upstream.astype(BF16)
    upstream_low = lay.gather_tokens(upstream_own)
    mixed = route_back(after(result_low, upstream_own)).astype(BF16)

    act_grad = dot_back(upstream_low, down_weight)
    down_grad = dot_rows(act_low, upstream_low).astype(BF16)
    gate_grad, up_grad = act_back(act_grad)
    gate_up_low = jnp.concatenate([gate_grad.astype(BF16), up_grad.astype(BF16)], axis=1)
    ffn_in_grad, ffn_far = lay.scatter_tokens(
        lambda part: dot_back(part, gate_up_weight), gate_up_low
    )
    (hidden_part,) = ffn_norm_back(ffn_in_grad)
    hidden_grad = upstream + hidden_part
    hidden_own = hidden_grad.astype(BF16)
    gate_up_grad = dot_rows(ffn_in, gate_up_low).astype(BF16)

    hidden_low = lay.gather_tokens(hidden_own)
    out_w_grad = dot_rows(heads_out, hidden_low).astype(BF16)
    head_grad = dot_back(hidden_low, out_weight).astype(BF16).reshape(TP, rows, heads, HD)
    value_grad = jnp.einsum("bhrc,brhd->bcd", prob_low, head_grad, preferred_element_type=F32)
    prob_grad = jnp.einsum("brhd,bcd->bhrc", head_grad, value_rows, preferred_element_type=F32)
    score_grad = prob_rows * (prob_grad - jnp.sum(prob_rows * prob_grad, axis=-1, keepdims=True))
    score_low = score_grad.astype(BF16)
    query_grad = (
        jnp.einsum("bhrc,bcd->brhd", score_low, key_low, preferred_element_type=F32) * HD**-0.5
    )
    key_grad = (
        jnp.einsum("bhrc,brhd->bcd", score_low, query_low, preferred_element_type=F32) * HD**-0.5
    )
    q_raw_grad, k_raw_grad, q_gain_part, k_gain_part = prepare_back(
        (query_grad.reshape(all_rows, heads, HD), key_grad.reshape(all_rows, HD))
    )
    qkv_low = jnp.concatenate(
        [
            q_raw_grad.astype(BF16),
            k_raw_grad.astype(BF16),
            value_grad.astype(BF16).reshape(all_rows, HD),
        ],
        axis=1,
    )
    qkv_grad = dot_rows(normed, qkv_low).astype(BF16)

    gates = (qkv_grad, score_low, hidden_own, ffn_far)
    down_shard = lay.ring_scatter(down_grad.reshape(ring, ff_cols // ring, width), 0, gates)[0]
    gate_up_sum = lay.ring_scatter(
        gate_up_grad.reshape(TP, ring, gain_rows, 2 * ff_cols), 1, gates
    )

    attn_blocks = jnp.concatenate(
        [
            qkv_grad.reshape(TP, ring, gain_rows, qkv_cols)
            .transpose(1, 0, 2, 3)
            .reshape(ring, TP * gain_rows, qkv_cols),
            out_w_grad.reshape(ring, out_rows, width // 256, 256)
            .transpose(0, 2, 1, 3)
            .reshape(ring, out_rows * (width // 256), 256),
        ],
        axis=2,
    )
    attn_sum = lay.ring_scatter(attn_blocks, 0, ())[0]

    normed_grad, unused_sent = lay.scatter_tokens(lambda part: dot_back(part, qkv_weight), qkv_low)
    unused, attn_norm_back = jax.vjp(lambda v: norm_rows(v, attn_gain_all), inputs)
    packed_grad = hidden_grad + attn_norm_back(normed_grad)[0]

    small = jnp.concatenate(
        [q_gain_part, k_gain_part, loss_part[None], jnp.zeros((128 - 1,), F32)]
    )[None]
    bit = 1
    while bit < devices:
        small = small + lay.flip(small, bit)
        bit = bit * 2
    small = small[0]

    qkv_parts = lay.exchange(
        attn_sum[:, :qkv_cols].reshape(TP, gain_rows, qkv_cols).astype(BF16)
    )
    gate_up_parts = lay.exchange(
        gate_up_sum.reshape(TP, gain_rows, 2 * ff_cols).astype(BF16)
    )

    def whole(parts, first, last):
        return jnp.concatenate([part[:, first:last] for part in parts], axis=1).astype(F32)

    query_grad_shard = whole(qkv_parts, 0, q_cols)
    key_grad_shard = whole(qkv_parts, q_cols, q_cols + kv_cols)
    value_grad_shard = whole(qkv_parts, q_cols + kv_cols, qkv_cols)
    gate_grad_shard = whole(gate_up_parts, 0, ff_cols)
    up_grad_shard = whole(gate_up_parts, ff_cols, 2 * ff_cols)

    def gain_grad(gain, *pairs):
        total = 0.0
        for weight, grad in pairs:
            total = total + jnp.sum(weight.astype(F32) * grad, axis=1)
        return total / gain.astype(F32)

    attn_gain_shard = gain_grad(
        attn_gain,
        (w_query, query_grad_shard),
        (w_key, key_grad_shard),
        (w_value, value_grad_shard),
    )
    ffn_gain_shard = gain_grad(ffn_gain, (w_gate, gate_grad_shard), (w_up, up_grad_shard))
    out_shard = (
        attn_sum[:, qkv_cols:].reshape(width // 256, out_rows, 256).transpose(1, 0, 2)
    ).reshape(out_rows, width)
    return (
        mixed,
        small[2 * HD] / valid_count,
        route_back(packed_grad.astype(BF16)),
        attn_gain_shard,
        query_grad_shard,
        key_grad_shard,
        value_grad_shard,
        out_shard,
        small[:HD],
        small[HD : 2 * HD],
        ffn_gain_shard,
        gate_grad_shard,
        up_grad_shard,
        down_shard,
    )


def solution(mesh):
    rows = P(AXES, None)
    flat = P(AXES)
    in_specs = (rows, rows, rows, flat, rows, rows, rows, rows, P(), P(), flat)
    in_specs = in_specs + (rows, rows, rows, P(), rows, rows)
    out_specs = (rows, P(), rows, flat, rows, rows, rows, rows, P(), P(), flat, rows, rows, rows)
    return jax.shard_map(shards, mesh=mesh, in_specs=in_specs, out_specs=out_specs, check_vma=False)
```

```python
import jax
import jax.numpy as jnp
from jax import lax
from jax.sharding import PartitionSpec as P

KV_HEADS = 4
HD = 64
TP = 4
AXES = ("dp", "fsdp")

EPS = 1e-06
THETA = 10000.0
NEGATIVE = -1000000000.0

BF16 = jnp.bfloat16
F32 = jnp.float32


def segment_info(lengths, row_count):
    seq_ends = jnp.cumsum(lengths)
    seq_starts = seq_ends - lengths
    row_index = jnp.arange(row_count, dtype=jnp.int32)
    segment = jnp.sum((row_index[:, None] >= seq_ends[None, :]).astype(jnp.int32), axis=1)
    seg_first = jnp.concatenate([seq_starts, seq_ends[-1:]])
    labels = jnp.arange(seg_first.shape[0], dtype=jnp.int32)
    seg_begin = jnp.sum(
        jnp.where(segment[:, None] == labels[None, :], seg_first[None, :], 0), axis=1
    )
    allowed = (segment[:, None] == segment[None, :]) & (row_index[None, :] <= row_index[:, None])
    return (row_index - seg_begin, allowed, segment < lengths.shape[0])


def norm_rows(values, gain_vec):
    return values * lax.rsqrt(jnp.mean(values * values, axis=-1, keepdims=True) + EPS) * gain_vec


def rope_tables(positions, head_width):
    half_width = head_width // 2
    frequency = THETA ** (-(jnp.arange(half_width, dtype=F32) * 2.0) / head_width)
    angles = positions.astype(F32)[:, None] * frequency[None, :]
    return (jnp.cos(angles), jnp.sin(angles))


def rotate(values, cosine, sine_table):
    half_width = values.shape[-1] // 2
    front_half = values[..., :half_width]
    second = values[..., half_width:]
    return jnp.concatenate(
        [front_half * cosine - second * sine_table, front_half * sine_table + second * cosine],
        axis=-1,
    )


def swiglu(gate_rows, up_rows):
    return jax.nn.silu(gate_rows) * up_rows


def dot(left, right):
    return jnp.dot(left, right, preferred_element_type=F32)


def dot_rows(left, right):
    return jnp.einsum("ra,rb->ab", left, right, preferred_element_type=F32)


def dot_back(left, right):
    return jnp.einsum("ra,ba->rb", left, right, preferred_element_type=F32)


def after(value, *others):
    return lax.optimization_barrier((value,) + others)[0]


def tie(*values):
    return lax.optimization_barrier(values)


class Layout:
    def __init__(self, devices):
        self.devices = devices
        self.ring = devices // TP
        evens = list(range(0, self.ring, 2))
        odds = list(range(1, self.ring, 2))
        self.cycle = evens + odds[::-1]
        self.place = [self.cycle.index(g) for g in range(self.ring)]
        self.me = lax.axis_index("dp") * lax.axis_size("fsdp") + lax.axis_index("fsdp")
        self.t = self.me // self.ring
        self.g = self.me % self.ring
        half = self.g // 2
        self.pos = jnp.where(self.g == 2 * half, half, self.ring - 1 - half)

    def at(self, distance):
        index = self.pos + (distance % self.ring)
        index = jnp.where(index < self.ring, index, index - self.ring)
        return jnp.minimum(2 * index, 2 * self.ring - 1 - 2 * index)

    def swap(self, value, bit):
        pairs = [
            (t * self.ring + g, (t ^ bit) * self.ring + g)
            for t in range(TP)
            for g in range(self.ring)
        ]
        return lax.ppermute(value, AXES, pairs)

    def shift(self, value, step):
        pairs = [
            (t * self.ring + g, t * self.ring + self.cycle[(self.place[g] + step) % self.ring])
            for t in range(TP)
            for g in range(self.ring)
        ]
        return lax.ppermute(value, AXES, pairs)

    def flip(self, value, bit):
        return lax.ppermute(value, AXES, [(n, n ^ bit) for n in range(self.devices)])

    def gather_tokens(self, own):
        across = self.swap(own, 2)
        core = self.swap(own, 1)
        far = self.swap(across, 1)
        return jnp.concatenate([own, across, core, far], axis=0)

    def scatter_tokens(self, product, rows, hook=None):
        half = rows.shape[0] // 2
        own = half // 2
        sent = product(rows[half:]).astype(BF16)
        kept = product(rows[:half]) + self.swap(sent, 1).astype(F32)
        far = kept[own:].astype(BF16)
        if hook is not None:
            far = hook(far)
        return kept[:own] + self.swap(far, 2).astype(F32), far

    def exchange(self, pieces):
        got = []
        for bit in range(TP):
            piece = lax.dynamic_index_in_dim(pieces, self.t ^ bit, 0, keepdims=False)
            got.append(self.swap(piece, bit) if bit else piece)
        for bit in (1, 2):
            turned = (self.t & bit) != 0
            got = [jnp.where(turned, got[k ^ bit], got[k]) for k in range(TP)]
        return got

    def ring_gather(self, items, axes):
        count = len(items)
        fulls = []
        for item, axis in zip(items, axes):
            shape = list(item.shape)
            shape[axis] = self.ring
            full = jnp.zeros(tuple(shape), item.dtype)
            fulls.append(lax.dynamic_update_slice_in_dim(full, item, self.g, axis))
        rights = list(items)
        lefts = list(items)
        last = self.ring // 2
        for step in range(1, last):
            for k in range(count):
                rights[k] = self.shift(rights[k], 1)
                lefts[k] = self.shift(lefts[k], -1)
            if count > 1:
                token, rights[0], lefts[0] = tie(lax.create_token(), rights[0], lefts[0])
                for k in range(1, count):
                    rights[k], lefts[k] = tie(token, rights[k], lefts[k])[1:]
            for k in range(count):
                fulls[k] = lax.dynamic_update_slice_in_dim(
                    fulls[k], rights[k], self.at(-step), axes[k]
                )
                fulls[k] = lax.dynamic_update_slice_in_dim(
                    fulls[k], lefts[k], self.at(step), axes[k]
                )
        for k in range(count):
            item = items[k]
            split = 0 if axes[k] else 1
            half = item.shape[split] // 2
            first = self.shift(lax.slice_in_dim(rights[k], 0, half, axis=split), 1)
            second = self.shift(lax.slice_in_dim(lefts[k], half, 2 * half, axis=split), -1)
            start = [jnp.int32(0)] * item.ndim
            start[axes[k]] = self.at(last)
            full = lax.dynamic_update_slice(fulls[k], first, start)
            start[split] = jnp.int32(half)
            fulls[k] = lax.dynamic_update_slice(full, second, start)
        return fulls, tuple(rights) + tuple(lefts)

    def ring_scatter(self, full, axis, places, hook=tie):
        last = self.ring // 2

        def block(index):
            return lax.dynamic_slice_in_dim(full, index, 1, axis)

        split = 0 if axis else 1
        edge = block(self.at(last))
        half = edge.shape[split] // 2
        right = self.shift(lax.slice_in_dim(edge, 0, half, axis=split), 1)
        left = self.shift(lax.slice_in_dim(edge, half, 2 * half, axis=split), -1)
        pad = [(0, 0, 0)] * edge.ndim
        pad[split] = (0, half, 0)
        right = lax.pad(right, jnp.zeros((), BF16), pad)
        pad[split] = (half, 0, 0)
        left = lax.pad(left, jnp.zeros((), BF16), pad)
        for step in range(last - 1, 0, -1):
            ahead, behind = places[step]
            right = (block(ahead).astype(F32) + right.astype(F32)).astype(BF16)
            left = (block(behind).astype(F32) + left.astype(F32)).astype(BF16)
            right, left = hook(right, left)
            right = self.shift(right, 1)
            left = self.shift(left, -1)
        return block(self.g).astype(F32) + right.astype(F32) + left.astype(F32)

    def all_places(self):
        return [(self.at(k), self.at(-k)) for k in range(self.ring // 2)]


def shards(
    tokens,
    teacher,
    out_grad,
    attn_gain,
    w_query,
    w_key,
    w_value,
    w_out,
    query_gain,
    key_gain,
    ffn_gain,
    w_gate,
    w_up,
    w_down,
    seq_lengths,
    send_order,
    pack_order,
):
    groups = lax.axis_size("fsdp")
    devices = lax.axis_size("dp") * groups
    lay = Layout(devices)
    ring = lay.ring
    rows = tokens.shape[0]
    width = tokens.shape[1]
    gain_rows = attn_gain.shape[0]
    q_cols = w_query.shape[1] // TP
    kv_cols = w_key.shape[1] // TP
    qkv_cols = q_cols + 2 * kv_cols
    heads = q_cols // HD
    ff_cols = w_gate.shape[1] // TP
    out_rows = w_out.shape[0]
    all_rows = TP * rows

    my_lengths = seq_lengths[lay.me]
    valid_count = jnp.sum(seq_lengths).astype(F32)
    loss_ratio = float(devices * rows) / valid_count
    send_rows = send_order[0]
    pack_rows = pack_order[0]
    counting = jnp.arange(rows, dtype=jnp.int32)
    send_pick = (send_rows[:, None] == counting[None, :]).astype(BF16)
    pack_pick = (pack_rows[:, None] == counting[None, :]).astype(BF16)

    def to_all(values):
        return lax.all_to_all(values, "fsdp", split_axis=0, concat_axis=0, tiled=True)

    def route(values):
        sent = to_all(dot(send_pick, values).astype(BF16))
        return dot(pack_pick, sent).astype(BF16)

    def route_back(values):
        sent = to_all(dot_rows(pack_pick, values).astype(BF16))
        return dot_rows(send_pick, sent)

    pad_rows = 8
    qkv_pieces = jnp.concatenate(
        [
            w_query.reshape(gain_rows, TP, q_cols),
            w_key.reshape(gain_rows, TP, kv_cols),
            w_value.reshape(gain_rows, TP, kv_cols),
        ],
        axis=2,
    ).transpose(1, 0, 2)
    gain_line = jnp.concatenate(
        [
            jnp.pad(attn_gain, (0, 128 - gain_rows)),
            jnp.pad(ffn_gain, (0, 128 - gain_rows)),
            jnp.zeros((qkv_cols - 256,), BF16),
        ]
    )
    gain_block = jnp.broadcast_to(gain_line[None, None], (TP, pad_rows, qkv_cols))
    qkv_item = jnp.concatenate(
        lay.exchange(jnp.concatenate([qkv_pieces, gain_block], axis=1)), axis=0
    )
    item_rows = TP * (gain_rows + pad_rows)
    out_item = w_out.reshape(out_rows, width // 256, 256).transpose(1, 0, 2)
    out_item = out_item.reshape(out_rows * (width // 256), 256)
    out_item = jnp.pad(out_item, ((0, item_rows - out_item.shape[0]), (0, 0)))
    attn_item = jnp.concatenate([qkv_item, out_item], axis=1)
    (attn_full,), attn_sent = lay.ring_gather([attn_item[None]], [0])
    qkv_full = attn_full[:, :, :qkv_cols].reshape(ring, TP, gain_rows + pad_rows, qkv_cols)
    qkv_weight = qkv_full[:, :, :gain_rows].transpose(1, 0, 2, 3).reshape(width, qkv_cols)
    gain_full = qkv_full[:, :, gain_rows].transpose(1, 0, 2)
    attn_gain_all = gain_full[:, :, :gain_rows].reshape(width).astype(F32)
    ffn_gain_all = gain_full[:, :, 128 : 128 + gain_rows].reshape(width).astype(F32)
    out_weight = attn_full[:, : out_rows * (width // 256), qkv_cols:]
    out_weight = out_weight.reshape(ring, width // 256, out_rows, 256).transpose(0, 2, 1, 3)
    out_weight = out_weight.reshape(ring * out_rows, width)

    gate_up_pieces = jnp.concatenate(
        [w_gate.reshape(gain_rows, TP, ff_cols), w_up.reshape(gain_rows, TP, ff_cols)], axis=2
    ).transpose(1, 0, 2)
    gate_up_item = jnp.stack(lay.exchange(after(gate_up_pieces, qkv_item)))
    gate_up_item, down_item = lax.optimization_barrier((gate_up_item, w_down) + attn_sent)[:2]
    (gate_up_full, down_full), ffn_sent = lay.ring_gather(
        [gate_up_item[:, None], down_item[None]], [1, 0]
    )
    gate_up_weight = gate_up_full.reshape(width, 2 * ff_cols)
    down_weight = down_full.reshape(ff_cols, width)

    packed = route(tokens)
    loss_rows = route(after(jnp.concatenate([teacher, out_grad], axis=1), *ffn_sent))
    inputs = packed.astype(F32)
    group_rows = lay.gather_tokens(packed)
    teacher_rows = loss_rows[:, :width]
    seed_rows = loss_rows[:, width:]
    group_lengths = jnp.stack([seq_lengths[(lay.t ^ k) * ring + lay.g] for k in (0, 2, 1, 3)])
    positions, allowed, valid_group = jax.vmap(lambda ls: segment_info(ls, rows))(group_lengths)
    valid_rows = valid_group[0].astype(F32)
    cosine, sine_table = rope_tables(positions.reshape(all_rows), HD)

    def prepare(q_raw, k_raw, q_scale, k_scale):
        query = norm_rows(q_raw.reshape(all_rows, heads, HD), q_scale)
        key_rows = norm_rows(k_raw, k_scale)
        query = rotate(query, cosine[:, None, :], sine_table[:, None, :])
        return (query, rotate(key_rows, cosine, sine_table))

    normed = norm_rows(group_rows.astype(F32), attn_gain_all).astype(BF16)
    qkv = dot(normed, qkv_weight)
    value_rows = qkv[:, q_cols + kv_cols :].astype(BF16).reshape(TP, rows, HD)
    (query_rot, key_rot), prepare_back = jax.vjp(
        prepare,
        qkv[:, :q_cols],
        qkv[:, q_cols : q_cols + kv_cols],
        query_gain.astype(F32),
        key_gain.astype(F32),
    )
    query_low = query_rot.astype(BF16).reshape(TP, rows, heads, HD)
    key_low = key_rot.astype(BF16).reshape(TP, rows, HD)
    scores = (
        jnp.einsum("brhd,bcd->bhrc", query_low, key_low, preferred_element_type=F32) * HD**-0.5
    )
    scores = jnp.where(allowed[:, None], scores, NEGATIVE)
    log_total = jax.nn.logsumexp(scores, axis=-1)
    prob_rows = jnp.exp(scores - log_total[..., None])
    prob_low = prob_rows.astype(BF16)
    heads_out = jnp.einsum("bhrc,bcd->brhd", prob_low, value_rows, preferred_element_type=F32)
    heads_out = heads_out.reshape(all_rows, q_cols).astype(BF16)
    hidden_sum, unused_sent = lay.scatter_tokens(lambda part: dot(part, out_weight), heads_out)
    hidden = inputs + hidden_sum
    ffn_own, ffn_norm_back = jax.vjp(lambda v: norm_rows(v, ffn_gain_all), hidden)
    ffn_in = lay.gather_tokens(ffn_own.astype(BF16))
    gate_up = dot(ffn_in, gate_up_weight)
    act_value, act_back = jax.vjp(swiglu, gate_up[:, :ff_cols], gate_up[:, ff_cols:])
    act_low = act_value.astype(BF16)
    result_sum, unused_sent = lay.scatter_tokens(lambda part: dot(part, down_weight), act_low)
    result = hidden + result_sum
    result_low = result.astype(BF16)

    row_error = result_low.astype(F32) - teacher_rows.astype(F32)
    loss_part = jnp.sum(valid_rows * jnp.mean(row_error * row_error, axis=-1))
    upstream = seed_rows.astype(F32) + loss_ratio * valid_rows[:, None] * row_error
    upstream_own = upstream.astype(BF16)
    upstream_low = lay.gather_tokens(upstream_own)
    mixed = route_back(after(result_low, upstream_own)).astype(BF16)

    act_grad = dot_back(upstream_low, down_weight)
    down_grad = dot_rows(act_low, upstream_low).astype(BF16)
    gate_grad, up_grad = act_back(act_grad)
    gate_up_low = jnp.concatenate([gate_grad.astype(BF16), up_grad.astype(BF16)], axis=1)
    places = lay.all_places()

    def before(step, value):
        ahead, behind, value = tie(*places[step], value)
        places[step] = (ahead, behind)
        return value

    ffn_in_grad, ffn_far = lay.scatter_tokens(
        lambda part: dot_back(part, gate_up_weight), gate_up_low, None
    )
    (hidden_part,) = ffn_norm_back(ffn_in_grad)
    hidden_grad = upstream + hidden_part
    hidden_own = hidden_grad.astype(BF16)
    gate_up_grad = dot_rows(ffn_in, gate_up_low).astype(BF16)

    hidden_low = lay.gather_tokens(hidden_own)
    out_w_grad = dot_rows(heads_out, hidden_low).astype(BF16)
    head_grad = dot_back(hidden_low, out_weight).astype(BF16).reshape(TP, rows, heads, HD)
    value_grad = jnp.einsum("bhrc,brhd->bcd", prob_low, head_grad, preferred_element_type=F32)
    prob_grad = jnp.einsum("brhd,bcd->bhrc", head_grad, value_rows, preferred_element_type=F32)
    score_grad = prob_rows * (prob_grad - jnp.sum(prob_rows * prob_grad, axis=-1, keepdims=True))
    score_low = score_grad.astype(BF16)
    query_grad = (
        jnp.einsum("bhrc,bcd->brhd", score_low, key_low, preferred_element_type=F32) * HD**-0.5
    )
    key_grad = (
        jnp.einsum("bhrc,brhd->bcd", score_low, query_low, preferred_element_type=F32) * HD**-0.5
    )
    q_raw_grad, k_raw_grad, q_gain_part, k_gain_part = prepare_back(
        (query_grad.reshape(all_rows, heads, HD), key_grad.reshape(all_rows, HD))
    )
    qkv_low = jnp.concatenate(
        [
            q_raw_grad.astype(BF16),
            k_raw_grad.astype(BF16),
            value_grad.astype(BF16).reshape(all_rows, HD),
        ],
        axis=1,
    )
    qkv_grad = dot_rows(normed, qkv_low).astype(BF16)

    down_shard = lay.ring_scatter(down_grad.reshape(ring, ff_cols // ring, width), 0, places)[0]
    gate_up_sum = lay.ring_scatter(
        gate_up_grad.reshape(TP, ring, gain_rows, 2 * ff_cols), 1, places
    )

    attn_blocks = jnp.concatenate(
        [
            qkv_grad.reshape(TP, ring, gain_rows, qkv_cols)
            .transpose(1, 0, 2, 3)
            .reshape(ring, TP * gain_rows, qkv_cols),
            out_w_grad.reshape(ring, out_rows, width // 256, 256)
            .transpose(0, 2, 1, 3)
            .reshape(ring, out_rows * (width // 256), 256),
        ],
        axis=2,
    )
    attn_sum = lay.ring_scatter(attn_blocks, 0, lay.all_places())[0]
    normed_grad, unused_sent = lay.scatter_tokens(lambda part: dot_back(part, qkv_weight), qkv_low)
    unused, attn_norm_back = jax.vjp(lambda v: norm_rows(v, attn_gain_all), inputs)
    packed_grad = hidden_grad + attn_norm_back(normed_grad)[0]
    grad_rows = dot_rows(pack_pick, packed_grad.astype(BF16)).astype(BF16)

    small = jnp.concatenate(
        [q_gain_part, k_gain_part, loss_part[None], jnp.zeros((128 - 1,), F32)]
    )[None]
    bit = 1
    while bit < devices:
        small = small + lay.flip(small, bit)
        bit = bit * 2
    small = small[0]

    qkv_parts = lay.exchange(
        attn_sum[:, :qkv_cols].reshape(TP, gain_rows, qkv_cols).astype(BF16)
    )
    gate_up_parts = lay.exchange(
        gate_up_sum.reshape(TP, gain_rows, 2 * ff_cols).astype(BF16)
    )

    def whole(parts, first, last):
        return jnp.concatenate([part[:, first:last] for part in parts], axis=1).astype(F32)

    query_grad_shard = whole(qkv_parts, 0, q_cols)
    key_grad_shard = whole(qkv_parts, q_cols, q_cols + kv_cols)
    value_grad_shard = whole(qkv_parts, q_cols + kv_cols, qkv_cols)
    gate_grad_shard = whole(gate_up_parts, 0, ff_cols)
    up_grad_shard = whole(gate_up_parts, ff_cols, 2 * ff_cols)

    def gain_grad(gain, *pairs):
        total = 0.0
        for weight, grad in pairs:
            total = total + jnp.sum(weight.astype(F32) * grad, axis=1)
        return total / gain.astype(F32)

    attn_gain_shard = gain_grad(
        attn_gain,
        (w_query, query_grad_shard),
        (w_key, key_grad_shard),
        (w_value, value_grad_shard),
    )
    ffn_gain_shard = gain_grad(ffn_gain, (w_gate, gate_grad_shard), (w_up, up_grad_shard))
    out_shard = (
        attn_sum[:, qkv_cols:].reshape(width // 256, out_rows, 256).transpose(1, 0, 2)
    ).reshape(out_rows, width)
    return (
        mixed,
        small[2 * HD] / valid_count,
        dot_rows(send_pick, to_all(grad_rows)),
        attn_gain_shard,
        query_grad_shard,
        key_grad_shard,
        value_grad_shard,
        out_shard,
        small[:HD],
        small[HD : 2 * HD],
        ffn_gain_shard,
        gate_grad_shard,
        up_grad_shard,
        down_shard,
    )


def solution(mesh):
    rows = P(AXES, None)
    flat = P(AXES)
    in_specs = (rows, rows, rows, flat, rows, rows, rows, rows, P(), P(), flat)
    in_specs = in_specs + (rows, rows, rows, P(), rows, rows)
    out_specs = (rows, P(), rows, flat, rows, rows, rows, rows, P(), P(), flat, rows, rows, rows)
    return jax.shard_map(shards, mesh=mesh, in_specs=in_specs, out_specs=out_specs, check_vma=False)
```

```python
import jax
import jax.numpy as jnp
from jax import lax
from jax.sharding import PartitionSpec as P

KV_HEADS = 4
HD = 64
TP = 4
AXES = ("dp", "fsdp")

EPS = 1e-06
THETA = 10000.0
NEGATIVE = -1000000000.0

BF16 = jnp.bfloat16
F32 = jnp.float32


def segment_info(lengths, row_count):
    seq_ends = jnp.cumsum(lengths)
    seq_starts = seq_ends - lengths
    row_index = jnp.arange(row_count, dtype=jnp.int32)
    segment = jnp.sum((row_index[:, None] >= seq_ends[None, :]).astype(jnp.int32), axis=1)
    seg_first = jnp.concatenate([seq_starts, seq_ends[-1:]])
    labels = jnp.arange(seg_first.shape[0], dtype=jnp.int32)
    seg_begin = jnp.sum(
        jnp.where(segment[:, None] == labels[None, :], seg_first[None, :], 0), axis=1
    )
    allowed = (segment[:, None] == segment[None, :]) & (row_index[None, :] <= row_index[:, None])
    return (row_index - seg_begin, allowed, segment < lengths.shape[0])


def norm_rows(values, gain_vec):
    return values * lax.rsqrt(jnp.mean(values * values, axis=-1, keepdims=True) + EPS) * gain_vec


def rope_tables(positions, head_width):
    half_width = head_width // 2
    frequency = THETA ** (-(jnp.arange(half_width, dtype=F32) * 2.0) / head_width)
    angles = positions.astype(F32)[:, None] * frequency[None, :]
    return (jnp.cos(angles), jnp.sin(angles))


def rotate(values, cosine, sine_table):
    half_width = values.shape[-1] // 2
    front_half = values[..., :half_width]
    second = values[..., half_width:]
    return jnp.concatenate(
        [front_half * cosine - second * sine_table, front_half * sine_table + second * cosine],
        axis=-1,
    )


def swiglu(gate_rows, up_rows):
    return jax.nn.silu(gate_rows) * up_rows


def dot(left, right):
    return jnp.dot(left, right, preferred_element_type=F32)


def dot_rows(left, right):
    return jnp.einsum("ra,rb->ab", left, right, preferred_element_type=F32)


def dot_back(left, right):
    return jnp.einsum("ra,ba->rb", left, right, preferred_element_type=F32)


def after(value, *others):
    return lax.optimization_barrier((value,) + others)[0]


def tie(*values):
    return lax.optimization_barrier(values)


class Layout:
    def __init__(self, devices):
        self.devices = devices
        self.ring = devices // TP
        evens = list(range(0, self.ring, 2))
        odds = list(range(1, self.ring, 2))
        self.cycle = evens + odds[::-1]
        self.place = [self.cycle.index(g) for g in range(self.ring)]
        self.me = lax.axis_index("dp") * lax.axis_size("fsdp") + lax.axis_index("fsdp")
        self.t = self.me // self.ring
        self.g = self.me % self.ring
        half = self.g // 2
        self.pos = jnp.where(self.g == 2 * half, half, self.ring - 1 - half)

    def at(self, distance):
        index = self.pos + (distance % self.ring)
        index = jnp.where(index < self.ring, index, index - self.ring)
        return jnp.minimum(2 * index, 2 * self.ring - 1 - 2 * index)

    def swap(self, value, bit):
        pairs = [
            (t * self.ring + g, (t ^ bit) * self.ring + g)
            for t in range(TP)
            for g in range(self.ring)
        ]
        return lax.ppermute(value, AXES, pairs)

    def shift(self, value, step):
        pairs = [
            (t * self.ring + g, t * self.ring + self.cycle[(self.place[g] + step) % self.ring])
            for t in range(TP)
            for g in range(self.ring)
        ]
        return lax.ppermute(value, AXES, pairs)

    def flip(self, value, bit):
        return lax.ppermute(value, AXES, [(n, n ^ bit) for n in range(self.devices)])

    def gather_tokens(self, own):
        across = self.swap(own, 2)
        core = self.swap(own, 1)
        far = self.swap(across, 1)
        return jnp.concatenate([own, across, core, far], axis=0)

    def scatter_tokens(self, product, rows, hook=None):
        half = rows.shape[0] // 2
        own = half // 2
        sent = product(rows[half:]).astype(BF16)
        kept = product(rows[:half]) + self.swap(sent, 1).astype(F32)
        far = kept[own:].astype(BF16)
        if hook is not None:
            far = hook(far)
        return kept[:own] + self.swap(far, 2).astype(F32), far

    def exchange(self, pieces):
        got = []
        for bit in range(TP):
            piece = lax.dynamic_index_in_dim(pieces, self.t ^ bit, 0, keepdims=False)
            got.append(self.swap(piece, bit) if bit else piece)
        for bit in (1, 2):
            turned = (self.t & bit) != 0
            got = [jnp.where(turned, got[k ^ bit], got[k]) for k in range(TP)]
        return got

    def ring_gather(self, items, axes):
        count = len(items)
        fulls = []
        for item, axis in zip(items, axes):
            shape = list(item.shape)
            shape[axis] = self.ring
            full = jnp.zeros(tuple(shape), item.dtype)
            fulls.append(lax.dynamic_update_slice_in_dim(full, item, self.g, axis))
        rights = list(items)
        lefts = list(items)
        last = self.ring // 2
        for step in range(1, last):
            for k in range(count):
                rights[k] = self.shift(rights[k], 1)
                lefts[k] = self.shift(lefts[k], -1)
            if count > 1:
                token, rights[0], lefts[0] = tie(lax.create_token(), rights[0], lefts[0])
                for k in range(1, count):
                    rights[k], lefts[k] = tie(token, rights[k], lefts[k])[1:]
            for k in range(count):
                fulls[k] = lax.dynamic_update_slice_in_dim(
                    fulls[k], rights[k], self.at(-step), axes[k]
                )
                fulls[k] = lax.dynamic_update_slice_in_dim(
                    fulls[k], lefts[k], self.at(step), axes[k]
                )
        for k in range(count):
            item = items[k]
            split = 0 if axes[k] else 1
            half = item.shape[split] // 2
            first = self.shift(lax.slice_in_dim(rights[k], 0, half, axis=split), 1)
            second = self.shift(lax.slice_in_dim(lefts[k], half, 2 * half, axis=split), -1)
            start = [jnp.int32(0)] * item.ndim
            start[axes[k]] = self.at(last)
            full = lax.dynamic_update_slice(fulls[k], first, start)
            start[split] = jnp.int32(half)
            fulls[k] = lax.dynamic_update_slice(full, second, start)
        return fulls, tuple(rights) + tuple(lefts)

    def ring_scatter(self, full, axis, places, hook=tie):
        last = self.ring // 2

        def block(index):
            return lax.dynamic_slice_in_dim(full, index, 1, axis)

        split = 0 if axis else 1
        edge = block(self.at(last))
        half = edge.shape[split] // 2
        right = self.shift(lax.slice_in_dim(edge, 0, half, axis=split), 1)
        left = self.shift(lax.slice_in_dim(edge, half, 2 * half, axis=split), -1)
        pad = [(0, 0, 0)] * edge.ndim
        pad[split] = (0, half, 0)
        right = lax.pad(right, jnp.zeros((), BF16), pad)
        pad[split] = (half, 0, 0)
        left = lax.pad(left, jnp.zeros((), BF16), pad)
        for step in range(last - 1, 0, -1):
            ahead, behind = places[step]
            right = (block(ahead).astype(F32) + right.astype(F32)).astype(BF16)
            left = (block(behind).astype(F32) + left.astype(F32)).astype(BF16)
            right, left = hook(right, left)
            right = self.shift(right, 1)
            left = self.shift(left, -1)
        return block(self.g).astype(F32) + right.astype(F32) + left.astype(F32)

    def all_places(self):
        return [(self.at(k), self.at(-k)) for k in range(self.ring // 2)]


def shards(
    tokens,
    teacher,
    out_grad,
    attn_gain,
    w_query,
    w_key,
    w_value,
    w_out,
    query_gain,
    key_gain,
    ffn_gain,
    w_gate,
    w_up,
    w_down,
    seq_lengths,
    send_order,
    pack_order,
):
    groups = lax.axis_size("fsdp")
    devices = lax.axis_size("dp") * groups
    lay = Layout(devices)
    ring = lay.ring
    rows = tokens.shape[0]
    width = tokens.shape[1]
    gain_rows = attn_gain.shape[0]
    q_cols = w_query.shape[1] // TP
    kv_cols = w_key.shape[1] // TP
    qkv_cols = q_cols + 2 * kv_cols
    heads = q_cols // HD
    ff_cols = w_gate.shape[1] // TP
    out_rows = w_out.shape[0]
    all_rows = TP * rows

    my_lengths = seq_lengths[lay.me]
    valid_count = jnp.sum(seq_lengths).astype(F32)
    loss_ratio = float(devices * rows) / valid_count
    send_rows = send_order[0]
    pack_rows = pack_order[0]
    counting = jnp.arange(rows, dtype=jnp.int32)
    send_pick = (send_rows[:, None] == counting[None, :]).astype(BF16)
    pack_pick = (pack_rows[:, None] == counting[None, :]).astype(BF16)

    def to_all(values):
        return lax.all_to_all(values, "fsdp", split_axis=0, concat_axis=0, tiled=True)

    def route(values):
        sent = to_all(dot(send_pick, values).astype(BF16))
        return dot(pack_pick, sent).astype(BF16)

    def route_back(values):
        sent = to_all(dot_rows(pack_pick, values).astype(BF16))
        return dot_rows(send_pick, sent)

    pad_rows = 8
    qkv_pieces = jnp.concatenate(
        [
            w_query.reshape(gain_rows, TP, q_cols),
            w_key.reshape(gain_rows, TP, kv_cols),
            w_value.reshape(gain_rows, TP, kv_cols),
        ],
        axis=2,
    ).transpose(1, 0, 2)
    gain_line = jnp.concatenate(
        [
            jnp.pad(attn_gain, (0, 128 - gain_rows)),
            jnp.pad(ffn_gain, (0, 128 - gain_rows)),
            jnp.zeros((qkv_cols - 256,), BF16),
        ]
    )
    gain_block = jnp.broadcast_to(gain_line[None, None], (TP, pad_rows, qkv_cols))
    gate_up_pieces = jnp.concatenate(
        [w_gate.reshape(gain_rows, TP, ff_cols), w_up.reshape(gain_rows, TP, ff_cols)], axis=2
    ).transpose(1, 0, 2)
    both_pieces = jnp.concatenate(
        [
            jnp.concatenate([qkv_pieces, gain_block], axis=1),
            jnp.pad(gate_up_pieces, ((0, 0), (0, pad_rows), (0, 0))),
        ],
        axis=2,
    )
    both_items = lay.exchange(both_pieces)
    qkv_item = jnp.concatenate([item[:, :qkv_cols] for item in both_items], axis=0)
    item_rows = TP * (gain_rows + pad_rows)
    out_item = w_out.reshape(out_rows, width // 256, 256).transpose(1, 0, 2)
    out_item = out_item.reshape(out_rows * (width // 256), 256)
    out_item = jnp.pad(out_item, ((0, item_rows - out_item.shape[0]), (0, 0)))
    attn_item = jnp.concatenate([qkv_item, out_item], axis=1)
    (attn_full,), attn_sent = lay.ring_gather([attn_item[None]], [0])
    qkv_full = attn_full[:, :, :qkv_cols].reshape(ring, TP, gain_rows + pad_rows, qkv_cols)
    qkv_weight = qkv_full[:, :, :gain_rows].transpose(1, 0, 2, 3).reshape(width, qkv_cols)
    gain_full = qkv_full[:, :, gain_rows].transpose(1, 0, 2)
    attn_gain_all = gain_full[:, :, :gain_rows].reshape(width).astype(F32)
    ffn_gain_all = gain_full[:, :, 128 : 128 + gain_rows].reshape(width).astype(F32)
    out_weight = attn_full[:, : out_rows * (width // 256), qkv_cols:]
    out_weight = out_weight.reshape(ring, width // 256, out_rows, 256).transpose(0, 2, 1, 3)
    out_weight = out_weight.reshape(ring * out_rows, width)

    gate_up_item = jnp.stack([item[:gain_rows, qkv_cols:] for item in both_items])
    gate_up_item, down_item = lax.optimization_barrier((gate_up_item, w_down) + attn_sent)[:2]
    (gate_up_full, down_full), ffn_sent = lay.ring_gather(
        [gate_up_item[:, None], down_item[None]], [1, 0]
    )
    gate_up_weight = gate_up_full.reshape(width, 2 * ff_cols)
    down_weight = down_full.reshape(ff_cols, width)

    packed = route(tokens)
    loss_rows = route(after(jnp.concatenate([teacher, out_grad], axis=1), *ffn_sent))
    inputs = packed.astype(F32)
    group_rows = lay.gather_tokens(packed)
    teacher_rows = loss_rows[:, :width]
    seed_rows = loss_rows[:, width:]
    group_lengths = jnp.stack([seq_lengths[(lay.t ^ k) * ring + lay.g] for k in (0, 2, 1, 3)])
    positions, allowed, valid_group = jax.vmap(lambda ls: segment_info(ls, rows))(group_lengths)
    valid_rows = valid_group[0].astype(F32)
    cosine, sine_table = rope_tables(positions.reshape(all_rows), HD)

    def prepare(q_raw, k_raw, q_scale, k_scale):
        query = norm_rows(q_raw.reshape(all_rows, heads, HD), q_scale)
        key_rows = norm_rows(k_raw, k_scale)
        query = rotate(query, cosine[:, None, :], sine_table[:, None, :])
        return (query, rotate(key_rows, cosine, sine_table))

    normed = norm_rows(group_rows.astype(F32), attn_gain_all).astype(BF16)
    qkv = dot(normed, qkv_weight)
    value_rows = qkv[:, q_cols + kv_cols :].astype(BF16).reshape(TP, rows, HD)
    (query_rot, key_rot), prepare_back = jax.vjp(
        prepare,
        qkv[:, :q_cols],
        qkv[:, q_cols : q_cols + kv_cols],
        query_gain.astype(F32),
        key_gain.astype(F32),
    )
    query_low = query_rot.astype(BF16).reshape(TP, rows, heads, HD)
    key_low = key_rot.astype(BF16).reshape(TP, rows, HD)
    scores = (
        jnp.einsum("brhd,bcd->bhrc", query_low, key_low, preferred_element_type=F32) * HD**-0.5
    )
    scores = jnp.where(allowed[:, None], scores, NEGATIVE)
    log_total = jax.nn.logsumexp(scores, axis=-1)
    prob_rows = jnp.exp(scores - log_total[..., None])
    prob_low = prob_rows.astype(BF16)
    heads_out = jnp.einsum("bhrc,bcd->brhd", prob_low, value_rows, preferred_element_type=F32)
    heads_out = heads_out.reshape(all_rows, q_cols).astype(BF16)
    hidden_sum, unused_sent = lay.scatter_tokens(lambda part: dot(part, out_weight), heads_out)
    hidden = inputs + hidden_sum
    ffn_own, ffn_norm_back = jax.vjp(lambda v: norm_rows(v, ffn_gain_all), hidden)
    ffn_in = lay.gather_tokens(ffn_own.astype(BF16))
    gate_up = dot(ffn_in, gate_up_weight)
    act_value, act_back = jax.vjp(swiglu, gate_up[:, :ff_cols], gate_up[:, ff_cols:])
    act_low = act_value.astype(BF16)
    result_sum, unused_sent = lay.scatter_tokens(lambda part: dot(part, down_weight), act_low)
    result = hidden + result_sum
    result_low = result.astype(BF16)

    row_error = result_low.astype(F32) - teacher_rows.astype(F32)
    loss_part = jnp.sum(valid_rows * jnp.mean(row_error * row_error, axis=-1))
    upstream = seed_rows.astype(F32) + loss_ratio * valid_rows[:, None] * row_error
    upstream_own = upstream.astype(BF16)
    upstream_low = lay.gather_tokens(upstream_own)
    mixed = route_back(after(result_low, upstream_own)).astype(BF16)

    act_grad = dot_back(upstream_low, down_weight)
    down_grad = dot_rows(act_low, upstream_low).astype(BF16)
    gate_grad, up_grad = act_back(act_grad)
    gate_up_low = jnp.concatenate([gate_grad.astype(BF16), up_grad.astype(BF16)], axis=1)
    places = lay.all_places()

    def before(step, value):
        ahead, behind, value = tie(*places[step], value)
        places[step] = (ahead, behind)
        return value

    ffn_in_grad, ffn_far = lay.scatter_tokens(
        lambda part: dot_back(part, gate_up_weight), gate_up_low, None
    )
    (hidden_part,) = ffn_norm_back(ffn_in_grad)
    hidden_grad = upstream + hidden_part
    hidden_own = hidden_grad.astype(BF16)
    gate_up_grad = dot_rows(ffn_in, gate_up_low).astype(BF16)

    hidden_low = lay.gather_tokens(hidden_own)
    out_w_grad = dot_rows(heads_out, hidden_low).astype(BF16)
    head_grad = dot_back(hidden_low, out_weight).astype(BF16).reshape(TP, rows, heads, HD)
    value_grad = jnp.einsum("bhrc,brhd->bcd", prob_low, head_grad, preferred_element_type=F32)
    prob_grad = jnp.einsum("brhd,bcd->bhrc", head_grad, value_rows, preferred_element_type=F32)
    score_grad = prob_rows * (prob_grad - jnp.sum(prob_rows * prob_grad, axis=-1, keepdims=True))
    score_low = score_grad.astype(BF16)
    query_grad = (
        jnp.einsum("bhrc,bcd->brhd", score_low, key_low, preferred_element_type=F32) * HD**-0.5
    )
    key_grad = (
        jnp.einsum("bhrc,brhd->bcd", score_low, query_low, preferred_element_type=F32) * HD**-0.5
    )
    q_raw_grad, k_raw_grad, q_gain_part, k_gain_part = prepare_back(
        (query_grad.reshape(all_rows, heads, HD), key_grad.reshape(all_rows, HD))
    )
    qkv_low = jnp.concatenate(
        [
            q_raw_grad.astype(BF16),
            k_raw_grad.astype(BF16),
            value_grad.astype(BF16).reshape(all_rows, HD),
        ],
        axis=1,
    )
    qkv_grad = dot_rows(normed, qkv_low).astype(BF16)

    down_shard = lay.ring_scatter(down_grad.reshape(ring, ff_cols // ring, width), 0, places)[0]
    gate_up_sum = lay.ring_scatter(
        gate_up_grad.reshape(TP, ring, gain_rows, 2 * ff_cols), 1, places
    )

    attn_blocks = jnp.concatenate(
        [
            qkv_grad.reshape(TP, ring, gain_rows, qkv_cols)
            .transpose(1, 0, 2, 3)
            .reshape(ring, TP * gain_rows, qkv_cols),
            out_w_grad.reshape(ring, out_rows, width // 256, 256)
            .transpose(0, 2, 1, 3)
            .reshape(ring, out_rows * (width // 256), 256),
        ],
        axis=2,
    )
    attn_sum = lay.ring_scatter(attn_blocks, 0, lay.all_places())[0]
    normed_grad, unused_sent = lay.scatter_tokens(lambda part: dot_back(part, qkv_weight), qkv_low)
    unused, attn_norm_back = jax.vjp(lambda v: norm_rows(v, attn_gain_all), inputs)
    packed_grad = hidden_grad + attn_norm_back(normed_grad)[0]
    grad_rows = dot_rows(pack_pick, packed_grad.astype(BF16)).astype(BF16)

    small = jnp.concatenate(
        [q_gain_part, k_gain_part, loss_part[None], jnp.zeros((128 - 1,), F32)]
    )[None]
    bit = 1
    while bit < devices:
        small = small + lay.flip(small, bit)
        bit = bit * 2
    small = small[0]

    qkv_parts = lay.exchange(
        attn_sum[:, :qkv_cols].reshape(TP, gain_rows, qkv_cols).astype(BF16)
    )
    gate_up_parts = lay.exchange(
        gate_up_sum.reshape(TP, gain_rows, 2 * ff_cols).astype(BF16)
    )

    def whole(parts, first, last):
        return jnp.concatenate([part[:, first:last] for part in parts], axis=1).astype(F32)

    query_grad_shard = whole(qkv_parts, 0, q_cols)
    key_grad_shard = whole(qkv_parts, q_cols, q_cols + kv_cols)
    value_grad_shard = whole(qkv_parts, q_cols + kv_cols, qkv_cols)
    gate_grad_shard = whole(gate_up_parts, 0, ff_cols)
    up_grad_shard = whole(gate_up_parts, ff_cols, 2 * ff_cols)

    def gain_grad(gain, *pairs):
        total = 0.0
        for weight, grad in pairs:
            total = total + jnp.sum(weight.astype(F32) * grad, axis=1)
        return total / gain.astype(F32)

    attn_gain_shard = gain_grad(
        attn_gain,
        (w_query, query_grad_shard),
        (w_key, key_grad_shard),
        (w_value, value_grad_shard),
    )
    ffn_gain_shard = gain_grad(ffn_gain, (w_gate, gate_grad_shard), (w_up, up_grad_shard))
    out_shard = (
        attn_sum[:, qkv_cols:].reshape(width // 256, out_rows, 256).transpose(1, 0, 2)
    ).reshape(out_rows, width)
    return (
        mixed,
        small[2 * HD] / valid_count,
        dot_rows(send_pick, to_all(grad_rows)),
        attn_gain_shard,
        query_grad_shard,
        key_grad_shard,
        value_grad_shard,
        out_shard,
        small[:HD],
        small[HD : 2 * HD],
        ffn_gain_shard,
        gate_grad_shard,
        up_grad_shard,
        down_shard,
    )


def solution(mesh):
    rows = P(AXES, None)
    flat = P(AXES)
    in_specs = (rows, rows, rows, flat, rows, rows, rows, rows, P(), P(), flat)
    in_specs = in_specs + (rows, rows, rows, P(), rows, rows)
    out_specs = (rows, P(), rows, flat, rows, rows, rows, rows, P(), P(), flat, rows, rows, rows)
    return jax.shard_map(shards, mesh=mesh, in_specs=in_specs, out_specs=out_specs, check_vma=False)
```

```python
import jax
import jax.numpy as jnp
from jax import lax
from jax.sharding import PartitionSpec as P

KV_HEADS = 4
HD = 64
TP = 4
AXES = ("dp", "fsdp")

EPS = 1e-06
THETA = 10000.0
NEGATIVE = -1000000000.0

BF16 = jnp.bfloat16
F32 = jnp.float32


def segment_info(lengths, row_count):
    seq_ends = jnp.cumsum(lengths)
    seq_starts = seq_ends - lengths
    row_index = jnp.arange(row_count, dtype=jnp.int32)
    segment = jnp.sum((row_index[:, None] >= seq_ends[None, :]).astype(jnp.int32), axis=1)
    seg_first = jnp.concatenate([seq_starts, seq_ends[-1:]])
    labels = jnp.arange(seg_first.shape[0], dtype=jnp.int32)
    seg_begin = jnp.sum(
        jnp.where(segment[:, None] == labels[None, :], seg_first[None, :], 0), axis=1
    )
    allowed = (segment[:, None] == segment[None, :]) & (row_index[None, :] <= row_index[:, None])
    return (row_index - seg_begin, allowed, segment < lengths.shape[0])


def norm_rows(values, gain_vec):
    return values * lax.rsqrt(jnp.mean(values * values, axis=-1, keepdims=True) + EPS) * gain_vec


def rope_tables(positions, head_width):
    half_width = head_width // 2
    frequency = THETA ** (-(jnp.arange(half_width, dtype=F32) * 2.0) / head_width)
    angles = positions.astype(F32)[:, None] * frequency[None, :]
    return (jnp.cos(angles), jnp.sin(angles))


def rotate(values, cosine, sine_table):
    half_width = values.shape[-1] // 2
    front_half = values[..., :half_width]
    second = values[..., half_width:]
    return jnp.concatenate(
        [front_half * cosine - second * sine_table, front_half * sine_table + second * cosine],
        axis=-1,
    )


def swiglu(gate_rows, up_rows):
    return jax.nn.silu(gate_rows) * up_rows


def dot(left, right):
    return jnp.dot(left, right, preferred_element_type=F32)


def dot_rows(left, right):
    return jnp.einsum("ra,rb->ab", left, right, preferred_element_type=F32)


def dot_back(left, right):
    return jnp.einsum("ra,ba->rb", left, right, preferred_element_type=F32)


def after(value, *others):
    return lax.optimization_barrier((value,) + others)[0]


def tie(*values):
    return lax.optimization_barrier(values)


class Layout:
    def __init__(self, devices):
        self.devices = devices
        self.ring = devices // TP
        evens = list(range(0, self.ring, 2))
        odds = list(range(1, self.ring, 2))
        self.cycle = evens + odds[::-1]
        self.place = [self.cycle.index(g) for g in range(self.ring)]
        self.me = lax.axis_index("dp") * lax.axis_size("fsdp") + lax.axis_index("fsdp")
        self.t = self.me // self.ring
        self.g = self.me % self.ring
        half = self.g // 2
        self.pos = jnp.where(self.g == 2 * half, half, self.ring - 1 - half)

    def at(self, distance):
        index = self.pos + (distance % self.ring)
        index = jnp.where(index < self.ring, index, index - self.ring)
        return jnp.minimum(2 * index, 2 * self.ring - 1 - 2 * index)

    def swap(self, value, bit):
        pairs = [
            (t * self.ring + g, (t ^ bit) * self.ring + g)
            for t in range(TP)
            for g in range(self.ring)
        ]
        return lax.ppermute(value, AXES, pairs)

    def shift(self, value, step):
        pairs = [
            (t * self.ring + g, t * self.ring + self.cycle[(self.place[g] + step) % self.ring])
            for t in range(TP)
            for g in range(self.ring)
        ]
        return lax.ppermute(value, AXES, pairs)

    def flip(self, value, bit):
        return lax.ppermute(value, AXES, [(n, n ^ bit) for n in range(self.devices)])

    def gather_tokens(self, own):
        across = self.swap(own, 2)
        core = self.swap(own, 1)
        far = self.swap(across, 1)
        return jnp.concatenate([own, across, core, far], axis=0)

    def scatter_tokens(self, product, rows, hook=None):
        half = rows.shape[0] // 2
        own = half // 2
        sent = product(rows[half:]).astype(BF16)
        kept = product(rows[:half]) + self.swap(sent, 1).astype(F32)
        far = kept[own:].astype(BF16)
        if hook is not None:
            far = hook(far)
        return kept[:own] + self.swap(far, 2).astype(F32), far

    def exchange(self, pieces):
        got = []
        for bit in range(TP):
            piece = lax.dynamic_index_in_dim(pieces, self.t ^ bit, 0, keepdims=False)
            got.append(self.swap(piece, bit) if bit else piece)
        for bit in (1, 2):
            turned = (self.t & bit) != 0
            got = [jnp.where(turned, got[k ^ bit], got[k]) for k in range(TP)]
        return got

    def ring_gather(self, items, axes):
        count = len(items)
        fulls = []
        for item, axis in zip(items, axes):
            shape = list(item.shape)
            shape[axis] = self.ring
            full = jnp.zeros(tuple(shape), item.dtype)
            fulls.append(lax.dynamic_update_slice_in_dim(full, item, self.g, axis))
        rights = list(items)
        lefts = list(items)
        last = self.ring // 2
        for step in range(1, last):
            for k in range(count):
                rights[k] = self.shift(rights[k], 1)
                lefts[k] = self.shift(lefts[k], -1)
            if count > 1:
                token, rights[0], lefts[0] = tie(lax.create_token(), rights[0], lefts[0])
                for k in range(1, count):
                    rights[k], lefts[k] = tie(token, rights[k], lefts[k])[1:]
            for k in range(count):
                fulls[k] = lax.dynamic_update_slice_in_dim(
                    fulls[k], rights[k], self.at(-step), axes[k]
                )
                fulls[k] = lax.dynamic_update_slice_in_dim(
                    fulls[k], lefts[k], self.at(step), axes[k]
                )
        for k in range(count):
            item = items[k]
            split = 0 if axes[k] else 1
            half = item.shape[split] // 2
            first = self.shift(lax.slice_in_dim(rights[k], 0, half, axis=split), 1)
            second = self.shift(lax.slice_in_dim(lefts[k], half, 2 * half, axis=split), -1)
            start = [jnp.int32(0)] * item.ndim
            start[axes[k]] = self.at(last)
            full = lax.dynamic_update_slice(fulls[k], first, start)
            start[split] = jnp.int32(half)
            fulls[k] = lax.dynamic_update_slice(full, second, start)
        return fulls, tuple(rights) + tuple(lefts)

    def ring_scatter(self, full, axis, places, hook=tie):
        last = self.ring // 2

        def block(index):
            return lax.dynamic_slice_in_dim(full, index, 1, axis)

        split = 0 if axis else 1
        edge = block(self.at(last))
        half = edge.shape[split] // 2
        right = self.shift(lax.slice_in_dim(edge, 0, half, axis=split), 1)
        left = self.shift(lax.slice_in_dim(edge, half, 2 * half, axis=split), -1)
        pad = [(0, 0, 0)] * edge.ndim
        pad[split] = (0, half, 0)
        right = lax.pad(right, jnp.zeros((), BF16), pad)
        pad[split] = (half, 0, 0)
        left = lax.pad(left, jnp.zeros((), BF16), pad)
        for step in range(last - 1, 0, -1):
            ahead, behind = places[step]
            right = (block(ahead).astype(F32) + right.astype(F32)).astype(BF16)
            left = (block(behind).astype(F32) + left.astype(F32)).astype(BF16)
            right, left = hook(right, left)
            right = self.shift(right, 1)
            left = self.shift(left, -1)
        return block(self.g).astype(F32) + right.astype(F32) + left.astype(F32)

    def all_places(self):
        return [(self.at(k), self.at(-k)) for k in range(self.ring // 2)]


def shards(
    tokens,
    teacher,
    out_grad,
    attn_gain,
    w_query,
    w_key,
    w_value,
    w_out,
    query_gain,
    key_gain,
    ffn_gain,
    w_gate,
    w_up,
    w_down,
    seq_lengths,
    send_order,
    pack_order,
):
    groups = lax.axis_size("fsdp")
    devices = lax.axis_size("dp") * groups
    lay = Layout(devices)
    ring = lay.ring
    rows = tokens.shape[0]
    width = tokens.shape[1]
    gain_rows = attn_gain.shape[0]
    q_cols = w_query.shape[1] // TP
    kv_cols = w_key.shape[1] // TP
    qkv_cols = q_cols + 2 * kv_cols
    heads = q_cols // HD
    ff_cols = w_gate.shape[1] // TP
    out_rows = w_out.shape[0]
    all_rows = TP * rows

    my_lengths = seq_lengths[lay.me]
    valid_count = jnp.sum(seq_lengths).astype(F32)
    loss_ratio = float(devices * rows) / valid_count
    send_rows = send_order[0]
    pack_rows = pack_order[0]
    counting = jnp.arange(rows, dtype=jnp.int32)
    send_pick = (send_rows[:, None] == counting[None, :]).astype(BF16)
    pack_pick = (pack_rows[:, None] == counting[None, :]).astype(BF16)

    def to_all(values):
        return lax.all_to_all(values, "fsdp", split_axis=0, concat_axis=0, tiled=True)

    def route(values):
        sent = to_all(dot(send_pick, values).astype(BF16))
        return dot(pack_pick, sent).astype(BF16)

    def route_back(values):
        sent = to_all(dot_rows(pack_pick, values).astype(BF16))
        return dot_rows(send_pick, sent)

    pad_rows = 8
    qkv_pieces = jnp.concatenate(
        [
            w_query.reshape(gain_rows, TP, q_cols),
            w_key.reshape(gain_rows, TP, kv_cols),
            w_value.reshape(gain_rows, TP, kv_cols),
        ],
        axis=2,
    ).transpose(1, 0, 2)
    gain_line = jnp.concatenate(
        [
            jnp.pad(attn_gain, (0, 128 - gain_rows)),
            jnp.pad(ffn_gain, (0, 128 - gain_rows)),
            jnp.zeros((qkv_cols - 256,), BF16),
        ]
    )
    gain_block = jnp.broadcast_to(gain_line[None, None], (TP, pad_rows, qkv_cols))
    qkv_item = jnp.concatenate(
        lay.exchange(jnp.concatenate([qkv_pieces, gain_block], axis=1)), axis=0
    )
    item_rows = TP * (gain_rows + pad_rows)
    out_item = w_out.reshape(out_rows, width // 256, 256).transpose(1, 0, 2)
    out_item = out_item.reshape(out_rows * (width // 256), 256)
    out_item = jnp.pad(out_item, ((0, item_rows - out_item.shape[0]), (0, 0)))
    attn_item = jnp.concatenate([qkv_item, out_item], axis=1)
    (attn_full,), attn_sent = lay.ring_gather([attn_item[None]], [0])
    qkv_full = attn_full[:, :, :qkv_cols].reshape(ring, TP, gain_rows + pad_rows, qkv_cols)
    qkv_weight = qkv_full[:, :, :gain_rows].transpose(1, 0, 2, 3).reshape(width, qkv_cols)
    gain_full = qkv_full[:, :, gain_rows].transpose(1, 0, 2)
    attn_gain_all = gain_full[:, :, :gain_rows].reshape(width).astype(F32)
    ffn_gain_all = gain_full[:, :, 128 : 128 + gain_rows].reshape(width).astype(F32)
    out_weight = attn_full[:, : out_rows * (width // 256), qkv_cols:]
    out_weight = out_weight.reshape(ring, width // 256, out_rows, 256).transpose(0, 2, 1, 3)
    out_weight = out_weight.reshape(ring * out_rows, width)

    gate_up_pieces = jnp.concatenate(
        [w_gate.reshape(gain_rows, TP, ff_cols), w_up.reshape(gain_rows, TP, ff_cols)], axis=2
    ).transpose(1, 0, 2)
    gate_up_item = jnp.stack(lay.exchange(after(gate_up_pieces, qkv_item)))
    gate_up_item, down_item = lax.optimization_barrier((gate_up_item, w_down) + attn_sent)[:2]
    (gate_up_full, down_full), ffn_sent = lay.ring_gather(
        [gate_up_item[:, None], down_item[None]], [1, 0]
    )
    gate_up_weight = gate_up_full.reshape(width, 2 * ff_cols)
    down_weight = down_full.reshape(ff_cols, width)

    packed = route(tokens)
    loss_rows = route(after(jnp.concatenate([teacher, out_grad], axis=1), *ffn_sent))
    inputs = packed.astype(F32)
    group_rows = lay.gather_tokens(packed)
    teacher_rows = loss_rows[:, :width]
    seed_rows = loss_rows[:, width:]
    group_lengths = jnp.stack([seq_lengths[(lay.t ^ k) * ring + lay.g] for k in (0, 2, 1, 3)])
    positions, allowed, valid_group = jax.vmap(lambda ls: segment_info(ls, rows))(group_lengths)
    valid_rows = valid_group[0].astype(F32)
    cosine, sine_table = rope_tables(positions.reshape(all_rows), HD)

    def prepare(q_raw, k_raw, q_scale, k_scale):
        query = norm_rows(q_raw.reshape(all_rows, heads, HD), q_scale)
        key_rows = norm_rows(k_raw, k_scale)
        query = rotate(query, cosine[:, None, :], sine_table[:, None, :])
        return (query, rotate(key_rows, cosine, sine_table))

    normed = norm_rows(group_rows.astype(F32), attn_gain_all).astype(BF16)
    qkv = dot(normed, qkv_weight)
    value_rows = qkv[:, q_cols + kv_cols :].astype(BF16).reshape(TP, rows, HD)
    (query_rot, key_rot), prepare_back = jax.vjp(
        prepare,
        qkv[:, :q_cols],
        qkv[:, q_cols : q_cols + kv_cols],
        query_gain.astype(F32),
        key_gain.astype(F32),
    )
    query_low = query_rot.astype(BF16).reshape(TP, rows, heads, HD)
    key_low = key_rot.astype(BF16).reshape(TP, rows, HD)
    scores = (
        jnp.einsum("brhd,bcd->bhrc", query_low, key_low, preferred_element_type=F32) * HD**-0.5
    )
    scores = jnp.where(allowed[:, None], scores, NEGATIVE)
    log_total = jax.nn.logsumexp(scores, axis=-1)
    prob_rows = jnp.exp(scores - log_total[..., None])
    prob_low = prob_rows.astype(BF16)
    heads_out = jnp.einsum("bhrc,bcd->brhd", prob_low, value_rows, preferred_element_type=F32)
    heads_out = heads_out.reshape(all_rows, q_cols).astype(BF16)
    hidden_sum, unused_sent = lay.scatter_tokens(lambda part: dot(part, out_weight), heads_out)
    hidden = inputs + hidden_sum
    ffn_own, ffn_norm_back = jax.vjp(lambda v: norm_rows(v, ffn_gain_all), hidden)
    ffn_in = lay.gather_tokens(ffn_own.astype(BF16))
    gate_up = dot(ffn_in, gate_up_weight)
    act_value, act_back = jax.vjp(swiglu, gate_up[:, :ff_cols], gate_up[:, ff_cols:])
    act_low = act_value.astype(BF16)
    result_sum, unused_sent = lay.scatter_tokens(lambda part: dot(part, down_weight), act_low)
    result = hidden + result_sum
    result_low = result.astype(BF16)

    row_error = result_low.astype(F32) - teacher_rows.astype(F32)
    loss_part = jnp.sum(valid_rows * jnp.mean(row_error * row_error, axis=-1))
    upstream = seed_rows.astype(F32) + loss_ratio * valid_rows[:, None] * row_error
    upstream_own = upstream.astype(BF16)
    upstream_low = lay.gather_tokens(upstream_own)
    mixed = route_back(after(result_low, upstream_own)).astype(BF16)

    act_grad = dot_back(upstream_low, down_weight)
    down_grad = dot_rows(act_low, upstream_low).astype(BF16)
    gate_grad, up_grad = act_back(act_grad)
    gate_up_low = jnp.concatenate([gate_grad.astype(BF16), up_grad.astype(BF16)], axis=1)
    places = lay.all_places()

    def before(step, value):
        ahead, behind, value = tie(*places[step], value)
        places[step] = (ahead, behind)
        return value

    ffn_in_grad, ffn_far = lay.scatter_tokens(
        lambda part: dot_back(part, gate_up_weight), gate_up_low, None
    )
    (hidden_part,) = ffn_norm_back(ffn_in_grad)
    hidden_grad = upstream + hidden_part
    hidden_own = hidden_grad.astype(BF16)
    gate_up_grad = dot_rows(ffn_in, gate_up_low).astype(BF16)

    hidden_low = lay.gather_tokens(hidden_own)
    out_w_grad = dot_rows(heads_out, hidden_low).astype(BF16)
    head_grad = dot_back(hidden_low, out_weight).astype(BF16).reshape(TP, rows, heads, HD)
    value_grad = jnp.einsum("bhrc,brhd->bcd", prob_low, head_grad, preferred_element_type=F32)
    prob_grad = jnp.einsum("brhd,bcd->bhrc", head_grad, value_rows, preferred_element_type=F32)
    score_grad = prob_rows * (prob_grad - jnp.sum(prob_rows * prob_grad, axis=-1, keepdims=True))
    score_low = score_grad.astype(BF16)
    query_grad = (
        jnp.einsum("bhrc,bcd->brhd", score_low, key_low, preferred_element_type=F32) * HD**-0.5
    )
    key_grad = (
        jnp.einsum("bhrc,brhd->bcd", score_low, query_low, preferred_element_type=F32) * HD**-0.5
    )
    q_raw_grad, k_raw_grad, q_gain_part, k_gain_part = prepare_back(
        (query_grad.reshape(all_rows, heads, HD), key_grad.reshape(all_rows, HD))
    )
    qkv_low = jnp.concatenate(
        [
            q_raw_grad.astype(BF16),
            k_raw_grad.astype(BF16),
            value_grad.astype(BF16).reshape(all_rows, HD),
        ],
        axis=1,
    )
    qkv_low = before(1, qkv_low)
    qkv_grad = dot_rows(normed, qkv_low).astype(BF16)

    down_shard = lay.ring_scatter(down_grad.reshape(ring, ff_cols // ring, width), 0, places)[0]
    gate_up_sum = lay.ring_scatter(
        gate_up_grad.reshape(TP, ring, gain_rows, 2 * ff_cols), 1, places
    )

    attn_blocks = jnp.concatenate(
        [
            qkv_grad.reshape(TP, ring, gain_rows, qkv_cols)
            .transpose(1, 0, 2, 3)
            .reshape(ring, TP * gain_rows, qkv_cols),
            out_w_grad.reshape(ring, out_rows, width // 256, 256)
            .transpose(0, 2, 1, 3)
            .reshape(ring, out_rows * (width // 256), 256),
        ],
        axis=2,
    )
    attn_sum = lay.ring_scatter(attn_blocks, 0, lay.all_places())[0]
    normed_grad, unused_sent = lay.scatter_tokens(lambda part: dot_back(part, qkv_weight), qkv_low)
    unused, attn_norm_back = jax.vjp(lambda v: norm_rows(v, attn_gain_all), inputs)
    packed_grad = hidden_grad + attn_norm_back(normed_grad)[0]
    grad_rows = dot_rows(pack_pick, packed_grad.astype(BF16)).astype(BF16)

    small = jnp.concatenate(
        [q_gain_part, k_gain_part, loss_part[None], jnp.zeros((128 - 1,), F32)]
    )[None]
    bit = 1
    while bit < devices:
        small = small + lay.flip(small, bit)
        bit = bit * 2
    small = small[0]

    qkv_parts = lay.exchange(
        attn_sum[:, :qkv_cols].reshape(TP, gain_rows, qkv_cols).astype(BF16)
    )
    gate_up_parts = lay.exchange(
        gate_up_sum.reshape(TP, gain_rows, 2 * ff_cols).astype(BF16)
    )

    def whole(parts, first, last):
        return jnp.concatenate([part[:, first:last] for part in parts], axis=1).astype(F32)

    query_grad_shard = whole(qkv_parts, 0, q_cols)
    key_grad_shard = whole(qkv_parts, q_cols, q_cols + kv_cols)
    value_grad_shard = whole(qkv_parts, q_cols + kv_cols, qkv_cols)
    gate_grad_shard = whole(gate_up_parts, 0, ff_cols)
    up_grad_shard = whole(gate_up_parts, ff_cols, 2 * ff_cols)

    def gain_grad(gain, *pairs):
        total = 0.0
        for weight, grad in pairs:
            total = total + jnp.sum(weight.astype(F32) * grad, axis=1)
        return total / gain.astype(F32)

    attn_gain_shard = gain_grad(
        attn_gain,
        (w_query, query_grad_shard),
        (w_key, key_grad_shard),
        (w_value, value_grad_shard),
    )
    ffn_gain_shard = gain_grad(ffn_gain, (w_gate, gate_grad_shard), (w_up, up_grad_shard))
    out_shard = (
        attn_sum[:, qkv_cols:].reshape(width // 256, out_rows, 256).transpose(1, 0, 2)
    ).reshape(out_rows, width)
    return (
        mixed,
        small[2 * HD] / valid_count,
        dot_rows(send_pick, to_all(grad_rows)),
        attn_gain_shard,
        query_grad_shard,
        key_grad_shard,
        value_grad_shard,
        out_shard,
        small[:HD],
        small[HD : 2 * HD],
        ffn_gain_shard,
        gate_grad_shard,
        up_grad_shard,
        down_shard,
    )


def solution(mesh):
    rows = P(AXES, None)
    flat = P(AXES)
    in_specs = (rows, rows, rows, flat, rows, rows, rows, rows, P(), P(), flat)
    in_specs = in_specs + (rows, rows, rows, P(), rows, rows)
    out_specs = (rows, P(), rows, flat, rows, rows, rows, rows, P(), P(), flat, rows, rows, rows)
    return jax.shard_map(shards, mesh=mesh, in_specs=in_specs, out_specs=out_specs, check_vma=False)
```
